512 devices in a mesh: seq: 128 (over y, z, x_lo), head: 4 (over x_hi, core).
Axes of the slice: x: 4 (x_hi: 2, x_lo: 2; x = x_hi * 2 + x_lo), y: 4, z: 16, core: 2. Of those that a mesh axis runs over, the one named last changes fastest.
Arguments:
- queries: bfloat16 [16384, 1024], P('seq', 'head'), may hold values from -16 to 16
- key_vectors: bfloat16 [16384, 1024], P('seq', 'head'), may hold values from -16 to 16
- values: bfloat16 [16384, 1024], P('seq', 'head'), may hold values from -6 to 6
- step_rates: float32 [16384, 4], P('seq', 'head'), may hold values from 0.1 to 1
- fast_weights: float32 [4, 3, 256, 256], P('head', None, 'seq'), may hold values from -0.375 to 0.375
- momentum: float32 [4, 3, 256, 256], P('head', None, 'seq'), may hold values from -0.4375 to 0.4375
- momentum_decay: float32 [4], P('head'), may hold values from 0.5 to 0.95
- memory_gain: float32 [1024], P('head'), may hold values from 0.5 to 1.5
- window_gain: float32 [1024], P('head'), may hold values from 0.5 to 1.5
Outputs:
- blended: bfloat16 [16384, 1024], P('seq', 'head')
- new_weights: float32 [4, 3, 256, 256], P('head', None, 'seq')
- new_momentum: float32 [4, 3, 256, 256], P('head', None, 'seq')
The draws below stay inside these ranges and needn't reach their ends.
All inputs are finite; a program needn't handle non-finite values.
Results may differ from the reference program's by a relative error of at most 0.0085.
Values may be sent and summed in bfloat16 or wider, within the bound.
No kernel may reach another device: no remote copies, remote signals or barrier semaphores. Data moves between devices by JAX's collectives and lax.ppermute only.
A program may use at most 64 MiB of HBM per device.

```python
import math
import jax
import jax.numpy as jnp
from jax import lax

DH = 256
HEADS = 4
WINDOW = 512
TOK_DEV = 128
TOKENS = 16384
D = 1024


def drawn_pair(key):
    base_key = jax.random.fold_in(key, 11)
    key_one, key_two = jax.random.split(base_key, 2)
    full_shape = (TOKENS, HEADS * DH)
    query_draw = jax.random.truncated_normal(key_one, -6.0, 6.0, full_shape, jnp.float32)
    key_draw = jax.random.truncated_normal(key_two, -6.0, 6.0, full_shape, jnp.float32)
    return (query_draw, key_draw)


def draw_queries(key, part):
    return drawn_pair(key)[0].astype(jnp.bfloat16)


def draw_key_vectors(key, part):
    return drawn_pair(key)[1].astype(jnp.bfloat16)


def block_scale(rng, dims, shards, smallest, high):
    def one(position, shards_of):
        steps = jax.random.uniform(jax.random.fold_in(jax.random.fold_in(rng, 6), position), (shards_of,), jnp.float32, smallest / len(shards), high / len(shards))
        return jnp.repeat(jnp.exp(steps), dims[position] // shards_of).reshape((-1,) + (1,) * (len(dims) - position - 1))

    level = one(*shards[0])
    for cut in shards[1:]:
        level = level * one(*cut)
    return level


def noise(stream_key, extent, deviation, limit, cuts=(), held_as=jnp.bfloat16):
    loudness = block_scale(stream_key, extent, cuts, -0.22, 0.18) if cuts else 1.0
    values = jax.random.normal(stream_key, extent, jnp.float32) * deviation * loudness
    return jnp.minimum(jnp.maximum(values, -limit), limit).astype(held_as)


def setup_inputs(seed: int = 0) -> dict:
    streams_of = jax.random.split(jax.random.key(seed), 10)
    return {
        "queries": draw_queries(jax.random.fold_in(streams_of[9], 71), 0),
        "key_vectors": draw_key_vectors(jax.random.fold_in(streams_of[9], 71), 0),
        "values": noise(streams_of[2], (TOKENS, D), 1.0, 6.0, ((0, 128), (1, 4))),
        "step_rates": jnp.clip(jnp.exp(math.log(1.0) - 2.3025851 * jax.random.uniform(streams_of[3], (TOKENS, HEADS), jnp.float32) ** block_scale(streams_of[3], (TOKENS, HEADS), ((0, 128), (1, 4)), -0.2, 0.2)), 0.1, 1.0),
        "fast_weights": noise(streams_of[4], (HEADS, 3, DH, DH), DH ** -0.5, 0.375, ((0, 4), (2, 128)), jnp.float32),
        "momentum": noise(streams_of[5], (HEADS, 3, DH, DH), 0.03, 0.4375, ((0, 4), (2, 128)), jnp.float32),
        "momentum_decay": jnp.clip(0.5 + 0.45 * jax.random.uniform(streams_of[6], (HEADS,), jnp.float32) ** block_scale(streams_of[6], (HEADS,), ((0, 4),), -0.2, 0.2), 0.5, 0.95),
        "memory_gain": jnp.clip(1.0 + 0.1 * jax.random.normal(streams_of[7], (D,), jnp.float32), 0.5, 1.5),
        "window_gain": jnp.clip(1.0 + 0.1 * jax.random.normal(streams_of[8], (D,), jnp.float32), 0.5, 1.5),
    }


def silu_slope(field):
    sigmoid_x = jax.nn.sigmoid(field)
    return sigmoid_x * (1.0 + field * (1.0 - sigmoid_x))

def keep_scale(candidate, previous):
    old_rms = jnp.sqrt(lax.optimization_barrier(jnp.mean(previous * previous, axis=-1, keepdims=True)) + 1e-06)
    new_rms = jnp.sqrt(lax.optimization_barrier(jnp.mean(candidate * candidate, axis=-1, keepdims=True)) + 1e-06)
    return candidate * (old_rms / new_rms)

def rms_scale(field, gain):
    return field * lax.rsqrt(lax.optimization_barrier(jnp.mean(field * field, axis=-1, keepdims=True)) + 1e-06) * gain

def window_attention(query_part, key_part, value_part):
    padded_keys = jnp.concatenate([jnp.zeros((WINDOW, DH), key_part.dtype), key_part], axis=0)
    padded_values = jnp.concatenate([jnp.zeros((WINDOW, DH), value_part.dtype), value_part], axis=0)
    block_count = TOKENS // TOK_DEV

    def one_block(block):
        first_row = (block * TOK_DEV).astype(jnp.int32)
        query_rows = lax.dynamic_slice_in_dim(query_part, first_row, TOK_DEV, 0)
        key_rows = lax.dynamic_slice_in_dim(padded_keys, first_row, TOK_DEV + WINDOW, 0)
        value_rows = lax.dynamic_slice_in_dim(padded_values, first_row, TOK_DEV + WINDOW, 0)
        scores = jnp.dot(query_rows, key_rows.T, preferred_element_type=jnp.float32) * DH ** (-0.5)
        query_pos = first_row + jnp.arange(TOK_DEV, dtype=jnp.int32)
        key_pos = first_row - WINDOW + jnp.arange(TOK_DEV + WINDOW, dtype=jnp.int32)
        distance = query_pos[:, None] - key_pos[None, :]
        allowed = (key_pos[None, :] >= 0) & (distance >= 0) & (distance < WINDOW)
        scores = jnp.where(allowed, scores, jnp.float32(-1e+30))
        row_max = lax.optimization_barrier(jnp.max(scores, axis=1, keepdims=True))
        weights = jnp.exp(scores - row_max)
        probabilities = (weights / lax.optimization_barrier(jnp.sum(weights, axis=1, keepdims=True))).astype(jnp.bfloat16)
        return jnp.dot(probabilities, value_rows, preferred_element_type=jnp.float32)
    blocks = lax.map(one_block, jnp.arange(block_count, dtype=jnp.int32))
    return blocks.reshape(TOKENS, DH)

def reference(queries, key_vectors, values, step_rates, fast_weights, momentum, momentum_decay, memory_gain, window_gain):
    inner_rate = 0.1 / math.sqrt(TOKENS)
    blended_heads = []
    weight_list = []
    moment_list = []
    for head_index in range(HEADS):
        low = head_index * DH
        query_part = queries[:, low:low + DH]
        key_part = key_vectors[:, low:low + DH]
        value_part = values[:, low:low + DH]
        rate_col = step_rates[:, head_index:head_index + 1]
        current = fast_weights[head_index]
        current_b = current.astype(jnp.bfloat16)
        gate_pre = jnp.dot(key_part, current_b[0], preferred_element_type=jnp.float32)
        up_pre = jnp.dot(key_part, current_b[1], preferred_element_type=jnp.float32)
        gate_act = jax.nn.silu(gate_pre)
        hidden = (gate_act * up_pre).astype(jnp.bfloat16)
        target_grad = (-(inner_rate * rate_col) * value_part.astype(jnp.float32)).astype(jnp.bfloat16)
        hidden_grad = jnp.dot(target_grad, current_b[2].T, preferred_element_type=jnp.float32)
        gate_grad = (hidden_grad * up_pre * silu_slope(gate_pre)).astype(jnp.bfloat16)
        up_grad = (hidden_grad * gate_act).astype(jnp.bfloat16)
        gradient = jnp.stack([jnp.dot(key_part.T, gate_grad, preferred_element_type=jnp.float32), jnp.dot(key_part.T, up_grad, preferred_element_type=jnp.float32), jnp.dot(hidden.T, target_grad, preferred_element_type=jnp.float32)])
        moment_new = momentum_decay[head_index] * momentum[head_index] + gradient
        weight_new = keep_scale(current - moment_new, current)
        updated = weight_new.astype(jnp.bfloat16)
        gate_out = jnp.dot(query_part, updated[0], preferred_element_type=jnp.float32)
        up_out = jnp.dot(query_part, updated[1], preferred_element_type=jnp.float32)
        inner_act = (jax.nn.silu(gate_out) * up_out).astype(jnp.bfloat16)
        recalled = jnp.dot(inner_act, updated[2], preferred_element_type=jnp.float32)
        attended = window_attention(query_part, key_part, value_part)
        joined = rms_scale(recalled, memory_gain[low:low + DH]) + rms_scale(attended, window_gain[low:low + DH])
        blended_heads.append(joined.astype(jnp.bfloat16))
        weight_list.append(weight_new)
        moment_list.append(moment_new)
    return (jnp.concatenate(blended_heads, axis=1), jnp.stack(weight_list), jnp.stack(moment_list))
```

```python
import math

import jax
import jax.numpy as jnp
from jax import lax
from jax.sharding import PartitionSpec as P

WINDOW = 512
Y_SIZE, Z_SIZE, X_SIZE = 4, 16, 2
NEAR_Z = 2
FAR = Z_SIZE // NEAR_Z
NEAR = Y_SIZE * NEAR_Z * X_SIZE
WIDTH = 256


def place(y, z, x):
    return (y * Z_SIZE + z) * X_SIZE + x


NEAR_GROUPS = [
    [
        place(y, k * NEAR_Z + p, x)
        for y in range(Y_SIZE)
        for p in range(NEAR_Z)
        for x in range(X_SIZE)
    ]
    for k in range(FAR)
]
FAR_GROUPS = [
    [place(y, k * NEAR_Z + p, x) for k in range(FAR)]
    for y in range(Y_SIZE)
    for p in range(NEAR_Z)
    for x in range(X_SIZE)
]


def exchange(blocks, groups):
    return lax.all_to_all(blocks, "seq", 0, 0, axis_index_groups=groups, tiled=True)


def spread(block, count, groups):
    return exchange(jnp.broadcast_to(block[None], (count,) + block.shape), groups)


def row_order():
    column = lax.broadcasted_iota(jnp.int32, (WIDTH, WIDTH), 1)
    row = lax.broadcasted_iota(jnp.int32, (WIDTH, WIDTH), 0)
    half, slot = column // 128, column % 128
    near, far = slot // FAR, slot % FAR
    x = near % X_SIZE
    p = (near // X_SIZE) % NEAR_Z
    y = near // (X_SIZE * NEAR_Z)
    device = (y * Z_SIZE + far * NEAR_Z + p) * X_SIZE + x
    return (row == 2 * device + half).astype(jnp.bfloat16)


def matmul(left, right):
    return jnp.dot(left, right, preferred_element_type=jnp.float32)


def matrix_of(whole, index):
    first = whole[:, index * 512 : index * 512 + 256]
    second = whole[:, index * 512 + 256 : index * 512 + 512]
    return jnp.concatenate([first, second], axis=0)


def rows_of(matrices):
    pieces = []
    for matrix in matrices:
        pieces += [matrix[:128], matrix[128:]]
    return jnp.concatenate(pieces, axis=1)


def silu_slope(field):
    sigmoid_x = jax.nn.sigmoid(field)
    return sigmoid_x * (1.0 + field * (1.0 - sigmoid_x))


def keep_scale(candidate, previous):
    old_rms = jnp.sqrt(jnp.mean(previous * previous, axis=-1, keepdims=True) + 1e-06)
    new_rms = jnp.sqrt(jnp.mean(candidate * candidate, axis=-1, keepdims=True) + 1e-06)
    return candidate * (old_rms / new_rms)


def rms_scale(field, gain):
    return field * lax.rsqrt(jnp.mean(field * field, axis=-1, keepdims=True) + 1e-06) * gain


def contract_rows(left, right):
    return lax.dot_general(
        left, right, (((0,), (0,)), ((), ())), preferred_element_type=jnp.float32
    )


def attention(queries, key_vectors, values, my_index):
    tokens_here, head_width = queries.shape
    seq_count = lax.axis_size("seq")
    both = jnp.concatenate([key_vectors, values], axis=0)
    earlier = [
        lax.ppermute(both, "seq", [(i, i + back) for i in range(seq_count - back)])
        for back in range(WINDOW // tokens_here, 0, -1)
    ]
    context_keys = jnp.concatenate([piece[:tokens_here] for piece in earlier] + [key_vectors], axis=0)
    context_values = jnp.concatenate([piece[tokens_here:] for piece in earlier] + [values], axis=0)
    scores = lax.dot_general(
        queries, context_keys, (((1,), (1,)), ((), ())), preferred_element_type=jnp.float32
    ) * head_width ** (-0.5)
    query_pos = my_index * tokens_here + jnp.arange(tokens_here, dtype=jnp.int32)
    key_pos = my_index * tokens_here - WINDOW + jnp.arange(tokens_here + WINDOW, dtype=jnp.int32)
    distance = query_pos[:, None] - key_pos[None, :]
    allowed = (key_pos[None, :] >= 0) & (distance >= 0) & (distance < WINDOW)
    scores = jnp.where(allowed, scores, jnp.float32(-1e30))
    row_max = jnp.max(scores, axis=1, keepdims=True)
    weights = jnp.exp(scores - row_max)
    probabilities = (weights / jnp.sum(weights, axis=1, keepdims=True)).astype(jnp.bfloat16)
    return matmul(probabilities, context_values)


def per_device(
    queries,
    key_vectors,
    values,
    step_rates,
    fast_weights,
    momentum,
    momentum_decay,
    memory_gain,
    window_gain,
):
    tokens_here = queries.shape[0]
    seq_count = lax.axis_size("seq")
    my_index = lax.axis_index("seq")
    my_far = ((my_index // X_SIZE) % Z_SIZE) // NEAR_Z
    inner_rate = 0.1 / math.sqrt(tokens_here * seq_count)
    decay = momentum_decay[0]
    attended = attention(queries, key_vectors, values, my_index)
    order = row_order()
    keys_ordered = matmul(key_vectors, order).astype(jnp.bfloat16)
    queries_ordered = matmul(queries, order).astype(jnp.bfloat16)

    own = jnp.concatenate(
        [fast_weights.reshape(1536), momentum.reshape(1536)]
    ).astype(jnp.bfloat16)
    line = spread(own, FAR, FAR_GROUPS)
    line_weights, line_moment = line[:, :1536], line[:, 1536:]
    whole = spread(line_weights, NEAR, NEAR_GROUPS).reshape(seq_count, 1536)
    gate_w, up_w = matrix_of(whole, 0), matrix_of(whole, 1)
    down_w = matmul(order, matrix_of(whole, 2)).astype(jnp.bfloat16)

    gate_pre = matmul(keys_ordered, gate_w)
    up_pre = matmul(keys_ordered, up_w)
    gate_act = jax.nn.silu(gate_pre)
    hidden = (gate_act * up_pre).astype(jnp.bfloat16)
    target_grad = (-(inner_rate * step_rates) * values.astype(jnp.float32)).astype(jnp.bfloat16)
    hidden_grad = lax.dot_general(
        target_grad, down_w, (((1,), (1,)), ((), ())), preferred_element_type=jnp.float32
    )
    gate_grad = (hidden_grad * up_pre * silu_slope(gate_pre)).astype(jnp.bfloat16)
    up_grad = (hidden_grad * gate_act).astype(jnp.bfloat16)
    hidden_ordered = matmul(hidden, order).astype(jnp.bfloat16)
    partial = rows_of(
        [
            contract_rows(keys_ordered, gate_grad),
            contract_rows(keys_ordered, up_grad),
            contract_rows(hidden_ordered, target_grad),
        ]
    ).astype(jnp.bfloat16)

    near_parts = exchange(partial.reshape(NEAR, FAR, 1536), NEAR_GROUPS)
    near_sum = jnp.sum(near_parts.astype(jnp.float32), axis=0).astype(jnp.bfloat16)
    far_parts = spread(near_sum, FAR, FAR_GROUPS)
    gradient = jnp.sum(far_parts.astype(jnp.float32), axis=0)

    def step(weights, moments, grads):
        count = grads.shape[0]
        weights = weights.astype(jnp.float32).reshape(count, 6, WIDTH)
        moments = moments.astype(jnp.float32).reshape(count, 6, WIDTH)
        moved = decay * moments + grads.reshape(count, 6, WIDTH)
        return keep_scale(weights - moved, weights), moved

    line_new = step(line_weights, line_moment, gradient)[0].astype(jnp.bfloat16)
    own_gradient = lax.dynamic_slice_in_dim(gradient, my_far, 1, 0)
    weight_new, moment_new = step(
        fast_weights.reshape(1, 1536), momentum.reshape(1, 1536), own_gradient
    )

    updated = spread(line_new.reshape(FAR, 1536), NEAR, NEAR_GROUPS).reshape(seq_count, 1536)
    gate_out = matmul(queries_ordered, matrix_of(updated, 0))
    up_out = matmul(queries_ordered, matrix_of(updated, 1))
    inner_act = (jax.nn.silu(gate_out) * up_out).astype(jnp.bfloat16)
    recalled = matmul(matmul(inner_act, order).astype(jnp.bfloat16), matrix_of(updated, 2))
    blended = (rms_scale(recalled, memory_gain) + rms_scale(attended, window_gain)).astype(
        jnp.bfloat16
    )
    return (
        blended,
        weight_new.reshape(fast_weights.shape),
        moment_new.reshape(momentum.shape),
    )


def solution(mesh):
    in_specs = (
        P("seq", "head"),
        P("seq", "head"),
        P("seq", "head"),
        P("seq", "head"),
        P("head", None, "seq", None),
        P("head", None, "seq", None),
        P("head"),
        P("head"),
        P("head"),
    )
    out_specs = (P("seq", "head"), P("head", None, "seq", None), P("head", None, "seq", None))
    return jax.shard_map(
        per_device, mesh=mesh, in_specs=in_specs, out_specs=out_specs, check_vma=False
    )
```

```python
import math

import jax
import jax.numpy as jnp
from jax import lax
from jax.experimental import pallas as pl
from jax.experimental.pallas import tpu as pltpu
from jax.sharding import PartitionSpec as P


WINDOW = 512
Y_SIZE, Z_SIZE, X_SIZE = 4, 16, 2
NEAR_Z = 2
FAR = Z_SIZE // NEAR_Z
NEAR = Y_SIZE * NEAR_Z * X_SIZE
WIDTH = 256
ROW = 6 * WIDTH
TOKENS_HERE = 128
BACK = WINDOW // TOKENS_HERE


def place(y, z, x):
    return (y * Z_SIZE + z) * X_SIZE + x


NEAR_GROUPS = [
    [
        place(y, k * NEAR_Z + p, x)
        for y in range(Y_SIZE)
        for p in range(NEAR_Z)
        for x in range(X_SIZE)
    ]
    for k in range(FAR)
]
FAR_GROUPS = [
    [place(y, k * NEAR_Z + p, x) for k in range(FAR)]
    for y in range(Y_SIZE)
    for p in range(NEAR_Z)
    for x in range(X_SIZE)
]


def exchange(blocks, groups):
    return lax.all_to_all(blocks, "seq", 0, 0, axis_index_groups=groups, tiled=True)


def row_order():
    column = lax.broadcasted_iota(jnp.int32, (WIDTH, WIDTH), 1)
    row = lax.broadcasted_iota(jnp.int32, (WIDTH, WIDTH), 0)
    half, slot = column // 128, column % 128
    near, far = slot // FAR, slot % FAR
    x = near % X_SIZE
    p = (near // X_SIZE) % NEAR_Z
    y = near // (X_SIZE * NEAR_Z)
    device = (y * Z_SIZE + far * NEAR_Z + p) * X_SIZE + x
    return (row == 2 * device + half).astype(jnp.bfloat16)


def matmul(left, right):
    return jnp.dot(left, right, preferred_element_type=jnp.float32)


def matrix_of(whole, index):
    first = whole[:, index * 512 : index * 512 + 256]
    second = whole[:, index * 512 + 256 : index * 512 + 512]
    return jnp.concatenate([first, second], axis=0)


def silu_slope(field, sigmoid_x):
    return sigmoid_x * (1.0 + field * (1.0 - sigmoid_x))


def row_rms(field):
    return jnp.sqrt(jnp.mean(field * field, axis=-1, keepdims=True) + 1e-06)


def rms_scale(field, gain):
    return field * lax.rsqrt(jnp.mean(field * field, axis=-1, keepdims=True) + 1e-06) * gain


def contract_rows(left, right):
    return lax.dot_general(
        left, right, (((0,), (0,)), ((), ())), preferred_element_type=jnp.float32
    )


def contract_columns(left, right):
    return lax.dot_general(
        left, right, (((1,), (1,)), ((), ())), preferred_element_type=jnp.float32
    )


def flat_rows(ref):
    return jnp.concatenate([ref[m, e : e + 1, :] for m in range(3) for e in range(2)], axis=1)


def pack_kernel(weights_ref, moments_ref, out_ref):
    both = jnp.concatenate([flat_rows(weights_ref), flat_rows(moments_ref)], axis=0)
    out_ref[...] = jnp.broadcast_to(both.astype(jnp.bfloat16)[None], out_ref.shape)


def relay_kernel(line_ref, spread_ref, kept_ref):
    line = line_ref[...].astype(jnp.float32)
    weights, moments = line[:, 0, :], line[:, 1, :]
    kept_ref[:, :ROW] = weights
    kept_ref[:, ROW:] = moments
    weights = weights.astype(jnp.bfloat16)
    for slot in range(NEAR):
        spread_ref[slot] = weights


def gradient_kernel(rate, keys_ref, values_ref, rates_ref, whole_ref, out_ref):
    order = row_order()
    keys = matmul(keys_ref[...], order).astype(jnp.bfloat16)
    target_grad = (-(rate * rates_ref[...]) * values_ref[...].astype(jnp.float32)).astype(
        jnp.bfloat16
    )
    gate_pre = matmul(keys, matrix_of(whole_ref, 0))
    up_pre = matmul(keys, matrix_of(whole_ref, 1))
    down = matmul(order, matrix_of(whole_ref, 2)).astype(jnp.bfloat16)
    sigmoid_x = jax.nn.sigmoid(gate_pre)
    gate_act = gate_pre * sigmoid_x
    hidden = (gate_act * up_pre).astype(jnp.bfloat16)
    hidden_grad = contract_columns(target_grad, down)
    gate_grad = (hidden_grad * up_pre * silu_slope(gate_pre, sigmoid_x)).astype(jnp.bfloat16)
    up_grad = (hidden_grad * gate_act).astype(jnp.bfloat16)
    hidden = matmul(hidden, order).astype(jnp.bfloat16)
    pairs = ((keys, gate_grad), (keys, up_grad), (hidden, target_grad))
    for index, (left, right) in enumerate(pairs):
        part = contract_rows(left, right).astype(jnp.bfloat16)
        out_ref[:, index * 512 : index * 512 + 256] = part[:128]
        out_ref[:, index * 512 + 256 : index * 512 + 512] = part[128:]


def near_sum_kernel(parts_ref, out_ref):
    total = parts_ref[0].astype(jnp.float32)
    for slot in range(1, NEAR):
        total += parts_ref[slot].astype(jnp.float32)
    total = total.astype(jnp.bfloat16)
    for slot in range(FAR):
        out_ref[slot] = total


def update_kernel(
    far_ref, decay_ref, parts_ref, kept_ref, weights_ref, moments_ref,
    spread_ref, weights_out, moments_out, gradient_ref,
):
    gradient = parts_ref[0].astype(jnp.float32)
    for slot in range(1, FAR):
        gradient += parts_ref[slot].astype(jnp.float32)
    gradient_ref[...] = gradient
    decay = decay_ref[0]
    pieces = []
    for index in range(6):
        columns = slice(index * WIDTH, (index + 1) * WIDTH)
        weights = kept_ref[:, columns]
        moments = kept_ref[:, ROW + index * WIDTH : ROW + (index + 1) * WIDTH]
        candidate = weights - (decay * moments + gradient[:, columns])
        pieces.append(candidate * (row_rms(weights) / row_rms(candidate)))
    renewed = jnp.concatenate(pieces, axis=1).astype(jnp.bfloat16)
    for slot in range(NEAR):
        spread_ref[slot] = renewed
    own = gradient_ref[pl.ds(far_ref[0], 1), :]
    for m in range(3):
        for e in range(2):
            index = 2 * m + e
            weights = weights_ref[m, e : e + 1, :]
            moved = decay * moments_ref[m, e : e + 1, :] + own[:, index * WIDTH : (index + 1) * WIDTH]
            candidate = weights - moved
            moments_out[m, e : e + 1, :] = moved
            weights_out[m, e : e + 1, :] = candidate * (row_rms(weights) / row_rms(candidate))


def attention_kernel(index_ref, queries_ref, keys_ref, values_ref, gain_ref, *rest):
    earlier, out_ref = rest[:BACK], rest[BACK]
    queries = queries_ref[...]
    my_index = index_ref[0]
    query = lax.broadcasted_iota(jnp.int32, (TOKENS_HERE, TOKENS_HERE), 0)
    key = lax.broadcasted_iota(jnp.int32, (TOKENS_HERE, TOKENS_HERE), 1)
    scores = []
    for piece, back in zip(earlier, range(BACK, 0, -1)):
        part = contract_columns(queries, piece[:TOKENS_HERE, :]) * WIDTH ** (-0.5)
        allowed = jnp.broadcast_to(my_index, key.shape) >= back
        if back == BACK:
            allowed = allowed & (key > query)
        scores.append(jnp.where(allowed, part, jnp.float32(-1e30)))
    part = contract_columns(queries, keys_ref[...]) * WIDTH ** (-0.5)
    scores.append(jnp.where(key <= query, part, jnp.float32(-1e30)))
    scores = jnp.concatenate(scores, axis=1)
    weights = jnp.exp(scores - jnp.max(scores, axis=1, keepdims=True))
    chances = (weights / jnp.sum(weights, axis=1, keepdims=True)).astype(jnp.bfloat16)
    context = jnp.concatenate([piece[TOKENS_HERE:, :] for piece in earlier] + [values_ref[...]], axis=0)
    out_ref[...] = rms_scale(matmul(chances, context), gain_ref[...])


def recall_kernel(queries_ref, whole_ref, attended_ref, gain_ref, out_ref):
    order = row_order()
    queries = matmul(queries_ref[...], order).astype(jnp.bfloat16)
    gate_out = matmul(queries, matrix_of(whole_ref, 0))
    up_out = matmul(queries, matrix_of(whole_ref, 1))
    inner_act = (gate_out * jax.nn.sigmoid(gate_out) * up_out).astype(jnp.bfloat16)
    inner_act = matmul(inner_act, order).astype(jnp.bfloat16)
    recalled = matmul(inner_act, matrix_of(whole_ref, 2))
    out_ref[...] = (rms_scale(recalled, gain_ref[...]) + attended_ref[...]).astype(jnp.bfloat16)


VMEM = pl.BlockSpec(memory_space=pltpu.VMEM)
SMEM = pl.BlockSpec(memory_space=pltpu.SMEM)


def call(kernel, outputs, specs, *arrays, scratch=(), flops=10**8):
    single = not isinstance(outputs, list)
    shapes = [jax.ShapeDtypeStruct(*output) for output in ([outputs] if single else outputs)]
    moved = sum(array.size * array.dtype.itemsize for array in arrays)
    result = pl.pallas_call(
        kernel,
        out_shape=shapes,
        in_specs=specs,
        out_specs=[VMEM] * len(shapes),
        scratch_shapes=scratch,
        compiler_params=pltpu.CompilerParams(vmem_limit_bytes=8 * 2**20),
        cost_estimate=pl.CostEstimate(flops=flops, bytes_accessed=moved, transcendentals=0),
    )(*arrays)
    return result[0] if single else result


def per_device(
    queries,
    key_vectors,
    values,
    step_rates,
    fast_weights,
    momentum,
    momentum_decay,
    memory_gain,
    window_gain,
):
    seq_count = lax.axis_size("seq")
    my_index = lax.axis_index("seq")
    my_far = ((my_index // X_SIZE) % Z_SIZE) // NEAR_Z
    inner_rate = 0.1 / math.sqrt(TOKENS_HERE * seq_count)
    own_weights, own_moments = fast_weights[0], momentum[0]
    bf16, f32 = jnp.bfloat16, jnp.float32

    packed = call(pack_kernel, ((FAR, 2, ROW), bf16), [VMEM] * 2, own_weights, own_moments)
    line = exchange(packed, FAR_GROUPS)
    sent, kept = call(relay_kernel, [((NEAR, FAR, ROW), bf16), ((FAR, 2 * ROW), f32)], [VMEM], line)
    whole = exchange(sent, NEAR_GROUPS).reshape(seq_count, ROW)
    partial = call(
        lambda *refs: gradient_kernel(inner_rate, *refs),
        ((seq_count, ROW), bf16),
        [VMEM] * 4,
        key_vectors, values, step_rates, whole,
    )
    near_parts = exchange(partial.reshape(NEAR, FAR, ROW), NEAR_GROUPS)
    near_sum = call(near_sum_kernel, ((FAR, FAR, ROW), bf16), [VMEM], near_parts)
    far_parts = exchange(near_sum, FAR_GROUPS)
    renewed, weight_new, moment_new = call(
        update_kernel,
        [((NEAR, FAR, ROW), bf16), ((3, 2, WIDTH), f32), ((3, 2, WIDTH), f32)],
        [SMEM, SMEM] + [VMEM] * 4,
        my_far.reshape(1), momentum_decay, far_parts, kept, own_weights, own_moments,
        scratch=[pltpu.VMEM((FAR, ROW), f32)],
    )
    updated = exchange(renewed, NEAR_GROUPS).reshape(seq_count, ROW)
    both = jnp.concatenate([key_vectors, values], axis=0)
    earlier = []
    for back in range(BACK, 0, -1):
        pairs = [(i, i + back) for i in range(seq_count - back)]
        earlier.append(lax.ppermute(both, "seq", pairs))
    attended = call(
        attention_kernel,
        ((TOKENS_HERE, WIDTH), f32),
        [SMEM] + [VMEM] * (4 + BACK),
        my_index.reshape(1), queries, key_vectors, values,
        window_gain.reshape(1, WIDTH), *earlier,
    )
    blended = call(
        recall_kernel,
        ((TOKENS_HERE, WIDTH), bf16),
        [VMEM] * 4,
        queries, updated, attended, memory_gain.reshape(1, WIDTH),
    )
    return blended, weight_new[None], moment_new[None]


def solution(mesh):
    in_specs = (
        P("seq", "head"),
        P("seq", "head"),
        P("seq", "head"),
        P("seq", "head"),
        P("head", None, "seq", None),
        P("head", None, "seq", None),
        P("head"),
        P("head"),
        P("head"),
    )
    out_specs = (P("seq", "head"), P("head", None, "seq", None), P("head", None, "seq", None))
    return jax.shard_map(
        per_device, mesh=mesh, in_specs=in_specs, out_specs=out_specs, check_vma=False
    )
```

```python
import math

import jax
import jax.numpy as jnp
from jax import lax
from jax.experimental import pallas as pl
from jax.experimental.pallas import tpu as pltpu
from jax.sharding import PartitionSpec as P


WINDOW = 512
Y_SIZE, Z_SIZE, X_SIZE = 4, 16, 2
NEAR_Z = 2
FAR = Z_SIZE // NEAR_Z
NEAR = Y_SIZE * NEAR_Z * X_SIZE
WIDTH = 256
ROW = 6 * WIDTH
TOKENS_HERE = 128
BACK = WINDOW // TOKENS_HERE


def place(y, z, x):
    return (y * Z_SIZE + z) * X_SIZE + x


NEAR_GROUPS = [
    [
        place(y, k * NEAR_Z + p, x)
        for y in range(Y_SIZE)
        for p in range(NEAR_Z)
        for x in range(X_SIZE)
    ]
    for k in range(FAR)
]
FAR_GROUPS = [
    [place(y, k * NEAR_Z + p, x) for k in range(FAR)]
    for y in range(Y_SIZE)
    for p in range(NEAR_Z)
    for x in range(X_SIZE)
]


def exchange(blocks, groups):
    return lax.all_to_all(blocks, "seq", 0, 0, axis_index_groups=groups, tiled=True)


def row_order():
    column = lax.broadcasted_iota(jnp.int32, (WIDTH, WIDTH), 1)
    row = lax.broadcasted_iota(jnp.int32, (WIDTH, WIDTH), 0)
    half, slot = column // 128, column % 128
    near, far = slot // FAR, slot % FAR
    x = near % X_SIZE
    p = (near // X_SIZE) % NEAR_Z
    y = near // (X_SIZE * NEAR_Z)
    device = (y * Z_SIZE + far * NEAR_Z + p) * X_SIZE + x
    return (row == 2 * device + half).astype(jnp.bfloat16)


def matmul(left, right):
    return jnp.dot(left, right, preferred_element_type=jnp.float32)


def matrix_of(whole, index):
    first = whole[:, index * 512 : index * 512 + 256]
    second = whole[:, index * 512 + 256 : index * 512 + 512]
    return jnp.concatenate([first, second], axis=0)


def silu_slope(field, sigmoid_x):
    return sigmoid_x * (1.0 + field * (1.0 - sigmoid_x))


def row_rms(field):
    return jnp.sqrt(jnp.mean(field * field, axis=-1, keepdims=True) + 1e-06)


def rms_scale(field, gain):
    return field * lax.rsqrt(jnp.mean(field * field, axis=-1, keepdims=True) + 1e-06) * gain


def contract_rows(left, right):
    return lax.dot_general(
        left, right, (((0,), (0,)), ((), ())), preferred_element_type=jnp.float32
    )


def contract_columns(left, right):
    return lax.dot_general(
        left, right, (((1,), (1,)), ((), ())), preferred_element_type=jnp.float32
    )


def flat_rows(ref):
    return jnp.concatenate([ref[m, e : e + 1, :] for m in range(3) for e in range(2)], axis=1)


def pack_kernel(
    weights_hbm, moments_hbm, keys_hbm, values_hbm, memory_hbm, window_hbm,
    out_ref, both_ref, weights_ref, moments_ref, memory_ref, window_ref, sems,
):
    moves = (
        (weights_hbm, weights_ref),
        (moments_hbm, moments_ref),
        (keys_hbm, both_ref.at[pl.ds(0, TOKENS_HERE)]),
        (values_hbm, both_ref.at[pl.ds(TOKENS_HERE, TOKENS_HERE)]),
        (memory_hbm, memory_ref),
        (window_hbm, window_ref),
    )
    copies = [
        pltpu.make_async_copy(source, target, sems.at[i])
        for i, (source, target) in enumerate(moves)
    ]
    for copy in copies:
        copy.start()
    copies[0].wait()
    copies[1].wait()
    both = jnp.concatenate([flat_rows(weights_ref), flat_rows(moments_ref)], axis=0)
    out_ref[...] = jnp.broadcast_to(both.astype(jnp.bfloat16)[None], out_ref.shape)
    for copy in copies[2:]:
        copy.wait()


def prepare_kernel(rate, both_ref, rates_ref, keys_out, target_out):
    keys_out[...] = matmul(both_ref[:TOKENS_HERE, :], row_order()).astype(jnp.bfloat16)
    rates = jnp.transpose(jnp.broadcast_to(rates_ref[...], (TOKENS_HERE, TOKENS_HERE)))
    scale = -(rate * jnp.concatenate([rates, rates], axis=1))
    target_out[...] = (scale * both_ref[TOKENS_HERE:, :].astype(jnp.float32)).astype(jnp.bfloat16)


def relay_kernel(line_ref, spread_ref, kept_ref):
    line = line_ref[...].astype(jnp.float32)
    weights, moments = line[:, 0, :], line[:, 1, :]
    kept_ref[:, :ROW] = weights
    kept_ref[:, ROW:] = moments
    weights = weights.astype(jnp.bfloat16)
    for slot in range(NEAR):
        spread_ref[slot] = weights


def gradient_kernel(keys_ref, target_ref, whole_ref, out_ref):
    order = row_order()
    keys, target_grad = keys_ref[...], target_ref[...]
    gate_pre = matmul(keys, matrix_of(whole_ref, 0))
    up_pre = matmul(keys, matrix_of(whole_ref, 1))
    down = matmul(order, matrix_of(whole_ref, 2)).astype(jnp.bfloat16)
    sigmoid_x = jax.nn.sigmoid(gate_pre)
    gate_act = gate_pre * sigmoid_x
    hidden = (gate_act * up_pre).astype(jnp.bfloat16)
    hidden_grad = contract_columns(target_grad, down)
    gate_grad = (hidden_grad * up_pre * silu_slope(gate_pre, sigmoid_x)).astype(jnp.bfloat16)
    up_grad = (hidden_grad * gate_act).astype(jnp.bfloat16)
    hidden = matmul(hidden, order).astype(jnp.bfloat16)
    pairs = ((keys, gate_grad), (keys, up_grad), (hidden, target_grad))
    for index, (left, right) in enumerate(pairs):
        part = contract_rows(left, right).astype(jnp.bfloat16)
        out_ref[:, index * 512 : index * 512 + 256] = part[:128]
        out_ref[:, index * 512 + 256 : index * 512 + 512] = part[128:]


def near_sum_kernel(parts_ref, out_ref):
    total = parts_ref[0].astype(jnp.float32)
    for slot in range(1, NEAR):
        total += parts_ref[slot].astype(jnp.float32)
    total = total.astype(jnp.bfloat16)
    for slot in range(FAR):
        out_ref[slot] = total


def update_kernel(far_ref, decay_ref, parts_ref, kept_ref, spread_ref, own_ref, gradient_ref):
    gradient = parts_ref[0].astype(jnp.float32)
    for slot in range(1, FAR):
        gradient += parts_ref[slot].astype(jnp.float32)
    gradient_ref[...] = gradient
    decay = decay_ref[0]
    pieces = []
    for index in range(6):
        columns = slice(index * WIDTH, (index + 1) * WIDTH)
        weights = kept_ref[:, columns]
        moments = kept_ref[:, ROW + index * WIDTH : ROW + (index + 1) * WIDTH]
        candidate = weights - (decay * moments + gradient[:, columns])
        pieces.append(candidate * (row_rms(weights) / row_rms(candidate)))
    renewed = jnp.concatenate(pieces, axis=1).astype(jnp.bfloat16)
    for slot in range(NEAR):
        spread_ref[slot] = renewed
    own_ref[...] = gradient_ref[pl.ds(far_ref[0], 1), :]


def attention_kernel(
    index_ref, queries_ref, both_ref, second_ref, fourth_ref, swapped_ref, gain_ref,
    out_ref, queries_out,
):
    queries = queries_ref[...]
    queries_out[...] = matmul(queries, row_order()).astype(jnp.bfloat16)
    my_index = index_ref[0]
    query = lax.broadcasted_iota(jnp.int32, (TOKENS_HERE, TOKENS_HERE), 0)
    key = lax.broadcasted_iota(jnp.int32, (TOKENS_HERE, TOKENS_HERE), 1)
    pieces = (
        (4, fourth_ref, 0),
        (3, swapped_ref, 2 * TOKENS_HERE),
        (2, second_ref, 0),
        (1, swapped_ref, 0),
        (0, both_ref, 0),
    )
    scores = []
    for back, ref, first in pieces:
        part = contract_columns(queries, ref[first : first + TOKENS_HERE, :]) * WIDTH ** (-0.5)
        allowed = jnp.broadcast_to(my_index, key.shape) >= back
        if back == BACK:
            allowed = allowed & (key > query)
        if back == 0:
            allowed = key <= query
        scores.append(jnp.where(allowed, part, jnp.float32(-1e30)))
    scores = jnp.concatenate(scores, axis=1)
    weights = jnp.exp(scores - jnp.max(scores, axis=1, keepdims=True))
    chances = (weights / jnp.sum(weights, axis=1, keepdims=True)).astype(jnp.bfloat16)
    context = jnp.concatenate(
        [ref[first + TOKENS_HERE : first + 2 * TOKENS_HERE, :] for _, ref, first in pieces], axis=0
    )
    out_ref[...] = rms_scale(matmul(chances, context), gain_ref[...])


def recall_kernel(
    decay_ref, own_ref, weights_ref, moments_ref, queries_ref, whole_ref, attended_ref, gain_ref,
    out_hbm, weights_hbm, moments_hbm, out_ref, weights_out, moments_out, sems,
):
    decay = decay_ref[0]
    for m in range(3):
        for e in range(2):
            first = (2 * m + e) * WIDTH
            weights = weights_ref[m, e : e + 1, :]
            moved = decay * moments_ref[m, e : e + 1, :] + own_ref[:, first : first + WIDTH]
            candidate = weights - moved
            moments_out[m, e : e + 1, :] = moved
            weights_out[m, e : e + 1, :] = candidate * (row_rms(weights) / row_rms(candidate))
    state = [
        pltpu.make_async_copy(weights_out, weights_hbm, sems.at[0]),
        pltpu.make_async_copy(moments_out, moments_hbm, sems.at[1]),
    ]
    for copy in state:
        copy.start()
    queries = queries_ref[...]
    gate_out = matmul(queries, matrix_of(whole_ref, 0))
    up_out = matmul(queries, matrix_of(whole_ref, 1))
    down = matmul(row_order(), matrix_of(whole_ref, 2)).astype(jnp.bfloat16)
    inner_act = (gate_out * jax.nn.sigmoid(gate_out) * up_out).astype(jnp.bfloat16)
    recalled = matmul(inner_act, down)
    out_ref[...] = (rms_scale(recalled, gain_ref[...]) + attended_ref[...]).astype(jnp.bfloat16)
    last = pltpu.make_async_copy(out_ref, out_hbm, sems.at[2])
    last.start()
    for copy in state:
        copy.wait()
    last.wait()


VMEM = pl.BlockSpec(memory_space=pltpu.VMEM)
SMEM = pl.BlockSpec(memory_space=pltpu.SMEM)
HBM = pl.BlockSpec(memory_space=pltpu.HBM)


def stay(array):
    return pltpu.with_memory_space_constraint(array, pltpu.HBM)


def call(kernel, outputs, specs, *arrays, out_spec=VMEM, scratch=(), flops=10**8):
    single = not isinstance(outputs, list)
    shapes = [jax.ShapeDtypeStruct(*output) for output in ([outputs] if single else outputs)]
    moved = sum(array.size * array.dtype.itemsize for array in arrays)
    result = pl.pallas_call(
        kernel,
        out_shape=shapes,
        in_specs=specs,
        out_specs=[out_spec] * len(shapes),
        scratch_shapes=scratch,
        compiler_params=pltpu.CompilerParams(vmem_limit_bytes=8 * 2**20),
        cost_estimate=pl.CostEstimate(flops=flops, bytes_accessed=moved, transcendentals=0),
    )(*arrays)
    return result[0] if single else result


def per_device(
    queries,
    key_vectors,
    values,
    step_rates,
    fast_weights,
    momentum,
    momentum_decay,
    memory_gain,
    window_gain,
):
    seq_count = lax.axis_size("seq")
    my_index = lax.axis_index("seq")
    my_far = ((my_index // X_SIZE) % Z_SIZE) // NEAR_Z
    inner_rate = 0.1 / math.sqrt(TOKENS_HERE * seq_count)
    bf16, f32 = jnp.bfloat16, jnp.float32
    block = ((3, 2, WIDTH), f32)
    line_gain = ((1, WIDTH), f32)

    packed, both, own_weights, own_moments, memory_row, window_row = call(
        pack_kernel,
        [((FAR, 2, ROW), bf16), ((2 * TOKENS_HERE, WIDTH), bf16), block, block, line_gain, line_gain],
        [HBM] * 6,
        *map(
            stay,
            (
                fast_weights[0], momentum[0], key_vectors, values,
                memory_gain.reshape(1, WIDTH), window_gain.reshape(1, WIDTH),
            ),
        ),
        scratch=[pltpu.SemaphoreType.DMA((6,))],
    )
    line = exchange(packed, FAR_GROUPS)
    second = lax.ppermute(both, "seq", [(i, i + 2) for i in range(seq_count - 2)])
    fourth = lax.ppermute(both, "seq", [(i, i + 4) for i in range(seq_count - 4)])
    keys, target_grad = call(
        lambda *refs: prepare_kernel(inner_rate, *refs),
        [((TOKENS_HERE, WIDTH), bf16)] * 2,
        [VMEM] * 2,
        both, step_rates.reshape(1, TOKENS_HERE),
    )
    sent, kept = call(relay_kernel, [((NEAR, FAR, ROW), bf16), ((FAR, 2 * ROW), f32)], [VMEM], line)
    whole = exchange(sent, NEAR_GROUPS).reshape(seq_count, ROW)
    partial = call(gradient_kernel, ((seq_count, ROW), bf16), [VMEM] * 3, keys, target_grad, whole)
    near_parts = exchange(partial.reshape(NEAR, FAR, ROW), NEAR_GROUPS)
    near_sum = call(near_sum_kernel, ((FAR, FAR, ROW), bf16), [VMEM], near_parts)
    far_parts = exchange(near_sum, FAR_GROUPS)
    odd = lax.rem(my_index, 2) == 1
    offered = jnp.where(
        odd,
        jnp.concatenate([second, fourth], axis=0),
        jnp.concatenate([both, second], axis=0),
    )
    swapped = lax.ppermute(offered, "seq", [(i, i ^ 1) for i in range(seq_count)])
    attended, queries_ordered = call(
        attention_kernel,
        [((TOKENS_HERE, WIDTH), f32), ((TOKENS_HERE, WIDTH), bf16)],
        [SMEM] + [VMEM] * 6,
        my_index.reshape(1), queries, both, second, fourth, swapped, window_row,
    )
    renewed, own_gradient = call(
        update_kernel,
        [((NEAR, FAR, ROW), bf16), ((1, ROW), f32)],
        [SMEM, SMEM] + [VMEM] * 2,
        my_far.reshape(1), momentum_decay, far_parts, kept,
        scratch=[pltpu.VMEM((FAR, ROW), f32)],
    )
    updated = exchange(renewed, NEAR_GROUPS).reshape(seq_count, ROW)
    blended, weight_new, moment_new = call(
        recall_kernel,
        [((TOKENS_HERE, WIDTH), bf16), block, block],
        [SMEM] + [VMEM] * 7,
        momentum_decay, own_gradient, own_weights, own_moments,
        queries_ordered, updated, attended, memory_row,
        out_spec=HBM,
        scratch=[
            pltpu.VMEM((TOKENS_HERE, WIDTH), bf16),
            pltpu.VMEM(*block),
            pltpu.VMEM(*block),
            pltpu.SemaphoreType.DMA((3,)),
        ],
    )
    return blended, weight_new[None], moment_new[None]


def solution(mesh):
    in_specs = (
        P("seq", "head"),
        P("seq", "head"),
        P("seq", "head"),
        P("seq", "head"),
        P("head", None, "seq", None),
        P("head", None, "seq", None),
        P("head"),
        P("head"),
        P("head"),
    )
    out_specs = (P("seq", "head"), P("head", None, "seq", None), P("head", None, "seq", None))
    return jax.shard_map(
        per_device, mesh=mesh, in_specs=in_specs, out_specs=out_specs, check_vma=False
    )
```

```python
import math

import jax
import jax.numpy as jnp
from jax import lax
from jax.experimental import pallas as pl
from jax.experimental.pallas import tpu as pltpu
from jax.sharding import PartitionSpec as P


WINDOW = 512
Y_SIZE, Z_SIZE, X_SIZE = 4, 16, 2
NEAR_Z = 2
FAR = Z_SIZE // NEAR_Z
NEAR = Y_SIZE * NEAR_Z * X_SIZE
WIDTH = 256
ROW = 6 * WIDTH
TOKENS_HERE = 128
BACK = WINDOW // TOKENS_HERE


def place(y, z, x):
    return (y * Z_SIZE + z) * X_SIZE + x


NEAR_GROUPS = [
    [
        place(y, k * NEAR_Z + p, x)
        for y in range(Y_SIZE)
        for p in range(NEAR_Z)
        for x in range(X_SIZE)
    ]
    for k in range(FAR)
]
FAR_GROUPS = [
    [place(y, k * NEAR_Z + p, x) for k in range(FAR)]
    for y in range(Y_SIZE)
    for p in range(NEAR_Z)
    for x in range(X_SIZE)
]


def exchange(blocks, groups):
    return lax.all_to_all(blocks, "seq", 0, 0, axis_index_groups=groups, tiled=True)


def row_order():
    column = lax.broadcasted_iota(jnp.int32, (WIDTH, WIDTH), 1)
    row = lax.broadcasted_iota(jnp.int32, (WIDTH, WIDTH), 0)
    half, slot = column // 128, column % 128
    near, far = slot // FAR, slot % FAR
    x = near % X_SIZE
    p = (near // X_SIZE) % NEAR_Z
    y = near // (X_SIZE * NEAR_Z)
    device = (y * Z_SIZE + far * NEAR_Z + p) * X_SIZE + x
    return (row == 2 * device + half).astype(jnp.bfloat16)


def matmul(left, right):
    return jnp.dot(left, right, preferred_element_type=jnp.float32)


def matrix_of(whole, index):
    first = whole[:, index * 512 : index * 512 + 256]
    second = whole[:, index * 512 + 256 : index * 512 + 512]
    return jnp.concatenate([first, second], axis=0)


def silu_slope(field, sigmoid_x):
    return sigmoid_x * (1.0 + field * (1.0 - sigmoid_x))


def row_rms(field):
    return jnp.sqrt(jnp.mean(field * field, axis=-1, keepdims=True) + 1e-06)


def rms_scale(field, gain):
    return field * lax.rsqrt(jnp.mean(field * field, axis=-1, keepdims=True) + 1e-06) * gain


def contract_rows(left, right):
    return lax.dot_general(
        left, right, (((0,), (0,)), ((), ())), preferred_element_type=jnp.float32
    )


def contract_columns(left, right):
    return lax.dot_general(
        left, right, (((1,), (1,)), ((), ())), preferred_element_type=jnp.float32
    )


def flat_rows(ref):
    return jnp.concatenate([ref[m, e : e + 1, :] for m in range(3) for e in range(2)], axis=1)


def send_all(stage_ref, out_hbm, sems):
    copies = [
        pltpu.make_async_copy(stage_ref, out_hbm.at[slot], sems.at[slot])
        for slot in range(out_hbm.shape[0])
    ]
    for copy in copies:
        copy.start()
    return copies


def pack_kernel(
    weights_hbm, moments_hbm, keys_hbm, values_hbm, memory_hbm, window_hbm,
    out_hbm, both_ref, weights_ref, moments_ref, memory_ref, window_ref, stage_ref, sems, out_sems,
):
    moves = (
        (weights_hbm, weights_ref),
        (moments_hbm, moments_ref),
        (keys_hbm, both_ref.at[pl.ds(0, TOKENS_HERE)]),
        (values_hbm, both_ref.at[pl.ds(TOKENS_HERE, TOKENS_HERE)]),
        (memory_hbm, memory_ref),
        (window_hbm, window_ref),
    )
    copies = [
        pltpu.make_async_copy(source, target, sems.at[i])
        for i, (source, target) in enumerate(moves)
    ]
    for copy in copies:
        copy.start()
    copies[0].wait()
    copies[1].wait()
    both = jnp.concatenate([flat_rows(weights_ref), flat_rows(moments_ref)], axis=0)
    stage_ref[...] = both.astype(jnp.bfloat16)
    for copy in send_all(stage_ref, out_hbm, out_sems) + copies[2:]:
        copy.wait()


def prepare_kernel(rate, both_ref, rates_ref, keys_out, target_out):
    keys_out[...] = matmul(both_ref[:TOKENS_HERE, :], row_order()).astype(jnp.bfloat16)
    rates = jnp.transpose(jnp.broadcast_to(rates_ref[...], (TOKENS_HERE, TOKENS_HERE)))
    scale = -(rate * jnp.concatenate([rates, rates], axis=1))
    target_out[...] = (scale * both_ref[TOKENS_HERE:, :].astype(jnp.float32)).astype(jnp.bfloat16)


def relay_kernel(line_ref, spread_ref, kept_ref):
    line = line_ref[...].astype(jnp.float32)
    weights, moments = line[:, 0, :], line[:, 1, :]
    kept_ref[:, :ROW] = weights
    kept_ref[:, ROW:] = moments
    weights = weights.astype(jnp.bfloat16)
    for slot in range(NEAR):
        spread_ref[slot] = weights


def natural_rows(slot, half):
    y, near = slot // (NEAR // Y_SIZE), slot % (NEAR // Y_SIZE)
    return pl.ds(y * 2 * Z_SIZE * X_SIZE + near * 2 + half, FAR, stride=NEAR // Y_SIZE * 2)


def natural_matrix(whole_ref, index, scratch_ref):
    for slot in range(NEAR):
        for half in range(2):
            first = (2 * index + half) * WIDTH
            part = whole_ref[slot * FAR : (slot + 1) * FAR, first : first + WIDTH]
            part = part.astype(jnp.float32)
            scratch_ref[0, natural_rows(slot, half), :] = part[:, :128]
            scratch_ref[1, natural_rows(slot, half), :] = part[:, 128:]
    return jnp.concatenate([scratch_ref[0], scratch_ref[1]], axis=1).astype(jnp.bfloat16)


def gradient_kernel(both_ref, keys_ref, target_ref, whole_ref, out_ref, down_ref, *sums):
    target_grad = target_ref[...]
    down = natural_matrix(whole_ref, 2, down_ref)
    gate_pre = matmul(keys_ref[...], matrix_of(whole_ref, 0))
    up_pre = matmul(keys_ref[...], matrix_of(whole_ref, 1))
    hidden_grad = contract_columns(target_grad, down)
    sigmoid_x = jax.nn.sigmoid(gate_pre)
    gate_act = gate_pre * sigmoid_x
    hidden = (gate_act * up_pre).astype(jnp.bfloat16)
    gate_grad = (hidden_grad * up_pre * silu_slope(gate_pre, sigmoid_x)).astype(jnp.bfloat16)
    up_grad = (hidden_grad * gate_act).astype(jnp.bfloat16)
    keys = both_ref[:TOKENS_HERE, :]
    pairs = ((hidden, target_grad), (keys, up_grad), (keys, gate_grad))
    for index, (left, right) in zip((2, 1, 0), pairs):
        total = contract_rows(left, right)
        sums[index][0] = total[:, :128]
        sums[index][1] = total[:, 128:]
        for slot in range(NEAR):
            for half in range(2):
                first = (2 * index + half) * WIDTH
                part = jnp.concatenate(
                    [sums[index][lane, natural_rows(slot, half), :] for lane in range(2)], axis=1
                )
                out_ref[slot * FAR : (slot + 1) * FAR, first : first + WIDTH] = part.astype(
                    jnp.bfloat16
                )


def near_sum_kernel(parts_ref, out_hbm, stage_ref, sems):
    total = parts_ref[0].astype(jnp.float32)
    for slot in range(1, NEAR):
        total += parts_ref[slot].astype(jnp.float32)
    stage_ref[...] = total.astype(jnp.bfloat16)
    for copy in send_all(stage_ref, out_hbm, sems):
        copy.wait()


def update_kernel(far_ref, decay_ref, parts_ref, kept_ref, spread_ref, own_ref, gradient_ref):
    gradient = parts_ref[0].astype(jnp.float32)
    for slot in range(1, FAR):
        gradient += parts_ref[slot].astype(jnp.float32)
    gradient_ref[...] = gradient
    decay = decay_ref[0]
    pieces = []
    for index in range(6):
        columns = slice(index * WIDTH, (index + 1) * WIDTH)
        weights = kept_ref[:, columns]
        moments = kept_ref[:, ROW + index * WIDTH : ROW + (index + 1) * WIDTH]
        candidate = weights - (decay * moments + gradient[:, columns])
        pieces.append(candidate * (row_rms(weights) / row_rms(candidate)))
    renewed = jnp.concatenate(pieces, axis=1).astype(jnp.bfloat16)
    for slot in range(NEAR):
        spread_ref[slot] = renewed
    own_ref[...] = gradient_ref[pl.ds(far_ref[0], 1), :]


def attention_kernel(
    index_ref, queries_ref, both_ref, second_ref, fourth_ref, swapped_ref, gain_ref,
    out_ref, queries_out,
):
    queries = queries_ref[...]
    queries_out[...] = matmul(queries, row_order()).astype(jnp.bfloat16)
    my_index = index_ref[0]
    query = lax.broadcasted_iota(jnp.int32, (TOKENS_HERE, TOKENS_HERE), 0)
    key = lax.broadcasted_iota(jnp.int32, (TOKENS_HERE, TOKENS_HERE), 1)
    pieces = (
        (4, fourth_ref, 0),
        (3, swapped_ref, 2 * TOKENS_HERE),
        (2, second_ref, 0),
        (1, swapped_ref, 0),
        (0, both_ref, 0),
    )
    scores = []
    for back, ref, first in pieces:
        part = contract_columns(queries, ref[first : first + TOKENS_HERE, :]) * WIDTH ** (-0.5)
        allowed = jnp.broadcast_to(my_index, key.shape) >= back
        if back == BACK:
            allowed = allowed & (key > query)
        if back == 0:
            allowed = key <= query
        scores.append(jnp.where(allowed, part, jnp.float32(-1e30)))
    scores = jnp.concatenate(scores, axis=1)
    weights = jnp.exp(scores - jnp.max(scores, axis=1, keepdims=True))
    chances = (weights / jnp.sum(weights, axis=1, keepdims=True)).astype(jnp.bfloat16)
    context = jnp.concatenate(
        [ref[first + TOKENS_HERE : first + 2 * TOKENS_HERE, :] for _, ref, first in pieces], axis=0
    )
    out_ref[...] = rms_scale(matmul(chances, context), gain_ref[...])


def recall_kernel(
    decay_ref, own_ref, weights_ref, moments_ref, queries_ref, whole_ref, attended_ref, gain_ref,
    out_hbm, weights_hbm, moments_hbm, out_ref, weights_out, moments_out, down_ref, sems,
):
    decay = decay_ref[0]
    for m in range(3):
        for e in range(2):
            first = (2 * m + e) * WIDTH
            weights = weights_ref[m, e : e + 1, :]
            moved = decay * moments_ref[m, e : e + 1, :] + own_ref[:, first : first + WIDTH]
            candidate = weights - moved
            moments_out[m, e : e + 1, :] = moved
            weights_out[m, e : e + 1, :] = candidate * (row_rms(weights) / row_rms(candidate))
    state = [
        pltpu.make_async_copy(weights_out, weights_hbm, sems.at[0]),
        pltpu.make_async_copy(moments_out, moments_hbm, sems.at[1]),
    ]
    for copy in state:
        copy.start()
    queries = queries_ref[...]
    gate_out = matmul(queries, matrix_of(whole_ref, 0))
    up_out = matmul(queries, matrix_of(whole_ref, 1))
    down = natural_matrix(whole_ref, 2, down_ref)
    inner_act = (gate_out * jax.nn.sigmoid(gate_out) * up_out).astype(jnp.bfloat16)
    recalled = matmul(inner_act, down)
    out_ref[...] = (rms_scale(recalled, gain_ref[...]) + attended_ref[...]).astype(jnp.bfloat16)
    last = pltpu.make_async_copy(out_ref, out_hbm, sems.at[2])
    last.start()
    for copy in state:
        copy.wait()
    last.wait()


VMEM = pl.BlockSpec(memory_space=pltpu.VMEM)
SMEM = pl.BlockSpec(memory_space=pltpu.SMEM)
HBM = pl.BlockSpec(memory_space=pltpu.HBM)


def stay(array):
    return pltpu.with_memory_space_constraint(array, pltpu.HBM)


def call(kernel, outputs, specs, *arrays, out_spec=VMEM, scratch=(), flops=10**8):
    single = not isinstance(outputs, list)
    shapes = [jax.ShapeDtypeStruct(*output) for output in ([outputs] if single else outputs)]
    moved = sum(array.size * array.dtype.itemsize for array in arrays)
    result = pl.pallas_call(
        kernel,
        out_shape=shapes,
        in_specs=specs,
        out_specs=out_spec if isinstance(out_spec, list) else [out_spec] * len(shapes),
        scratch_shapes=scratch,
        compiler_params=pltpu.CompilerParams(vmem_limit_bytes=8 * 2**20),
        cost_estimate=pl.CostEstimate(flops=flops, bytes_accessed=moved, transcendentals=0),
    )(*arrays)
    return result[0] if single else result


def per_device(
    queries,
    key_vectors,
    values,
    step_rates,
    fast_weights,
    momentum,
    momentum_decay,
    memory_gain,
    window_gain,
):
    seq_count = lax.axis_size("seq")
    my_index = lax.axis_index("seq")
    my_far = ((my_index // X_SIZE) % Z_SIZE) // NEAR_Z
    inner_rate = 0.1 / math.sqrt(TOKENS_HERE * seq_count)
    bf16, f32 = jnp.bfloat16, jnp.float32
    block = ((3, 2, WIDTH), f32)
    line_gain = ((1, WIDTH), f32)

    packed, both, own_weights, own_moments, memory_row, window_row = call(
        pack_kernel,
        [((FAR, 2, ROW), bf16), ((2 * TOKENS_HERE, WIDTH), bf16), block, block, line_gain, line_gain],
        [HBM] * 6,
        *map(
            stay,
            (
                fast_weights[0], momentum[0], key_vectors, values,
                memory_gain.reshape(1, WIDTH), window_gain.reshape(1, WIDTH),
            ),
        ),
        out_spec=[HBM] + [VMEM] * 5,
        scratch=[
            pltpu.VMEM((2, ROW), bf16),
            pltpu.SemaphoreType.DMA((6,)),
            pltpu.SemaphoreType.DMA((FAR,)),
        ],
    )
    line = exchange(packed, FAR_GROUPS)
    second = lax.ppermute(both, "seq", [(i, i + 2) for i in range(seq_count - 2)])
    fourth = lax.ppermute(both, "seq", [(i, i + 4) for i in range(seq_count - 4)])
    keys, target_grad = call(
        lambda *refs: prepare_kernel(inner_rate, *refs),
        [((TOKENS_HERE, WIDTH), bf16)] * 2,
        [VMEM] * 2,
        both, step_rates.reshape(1, TOKENS_HERE),
    )
    sent, kept = call(relay_kernel, [((NEAR, FAR, ROW), bf16), ((FAR, 2 * ROW), f32)], [VMEM], line)
    whole = exchange(sent, NEAR_GROUPS).reshape(seq_count, ROW)
    partial = call(
        gradient_kernel,
        ((seq_count, ROW), bf16),
        [VMEM] * 4,
        both, keys, target_grad, whole,
        scratch=[pltpu.VMEM((2, WIDTH, 128), f32)] * 4,
    )
    near_parts = exchange(partial.reshape(NEAR, FAR, ROW), NEAR_GROUPS)
    near_sum = call(
        near_sum_kernel,
        ((FAR, FAR, ROW), bf16),
        [VMEM],
        near_parts,
        out_spec=HBM,
        scratch=[pltpu.VMEM((FAR, ROW), bf16), pltpu.SemaphoreType.DMA((FAR,))],
    )
    far_parts = exchange(near_sum, FAR_GROUPS)
    odd = lax.rem(my_index, 2) == 1
    offered = jnp.where(
        odd,
        jnp.concatenate([second, fourth], axis=0),
        jnp.concatenate([both, second], axis=0),
    )
    swapped = lax.ppermute(offered, "seq", [(i, i ^ 1) for i in range(seq_count)])
    attended, queries_ordered = call(
        attention_kernel,
        [((TOKENS_HERE, WIDTH), f32), ((TOKENS_HERE, WIDTH), bf16)],
        [SMEM] + [VMEM] * 6,
        my_index.reshape(1), queries, both, second, fourth, swapped, window_row,
    )
    renewed, own_gradient = call(
        update_kernel,
        [((NEAR, FAR, ROW), bf16), ((1, ROW), f32)],
        [SMEM, SMEM] + [VMEM] * 2,
        my_far.reshape(1), momentum_decay, far_parts, kept,
        scratch=[pltpu.VMEM((FAR, ROW), f32)],
    )
    updated = exchange(renewed, NEAR_GROUPS).reshape(seq_count, ROW)
    blended, weight_new, moment_new = call(
        recall_kernel,
        [((TOKENS_HERE, WIDTH), bf16), block, block],
        [SMEM] + [VMEM] * 7,
        momentum_decay, own_gradient, own_weights, own_moments,
        queries_ordered, updated, attended, memory_row,
        out_spec=HBM,
        scratch=[
            pltpu.VMEM((TOKENS_HERE, WIDTH), bf16),
            pltpu.VMEM(*block),
            pltpu.VMEM(*block),
            pltpu.VMEM((2, WIDTH, 128), f32),
            pltpu.SemaphoreType.DMA((3,)),
        ],
    )
    return blended, weight_new[None], moment_new[None]


def solution(mesh):
    in_specs = (
        P("seq", "head"),
        P("seq", "head"),
        P("seq", "head"),
        P("seq", "head"),
        P("head", None, "seq", None),
        P("head", None, "seq", None),
        P("head"),
        P("head"),
        P("head"),
    )
    out_specs = (P("seq", "head"), P("head", None, "seq", None), P("head", None, "seq", None))
    return jax.shard_map(
        per_device, mesh=mesh, in_specs=in_specs, out_specs=out_specs, check_vma=False
    )
```

```python
import math

import jax
import jax.numpy as jnp
from jax import lax
from jax.experimental import pallas as pl
from jax.experimental.pallas import tpu as pltpu
from jax.sharding import PartitionSpec as P


WINDOW = 512
Y_SIZE, Z_SIZE, X_SIZE = 4, 16, 2
NEAR_Z = 2
FAR = Z_SIZE // NEAR_Z
NEAR = Y_SIZE * NEAR_Z * X_SIZE
WIDTH = 256
ROW = 6 * WIDTH
TOKENS_HERE = 128
BACK = WINDOW // TOKENS_HERE


def place(y, z, x):
    return (y * Z_SIZE + z) * X_SIZE + x


NEAR_GROUPS = [
    [
        place(y, k * NEAR_Z + p, x)
        for y in range(Y_SIZE)
        for p in range(NEAR_Z)
        for x in range(X_SIZE)
    ]
    for k in range(FAR)
]
FAR_GROUPS = [
    [place(y, k * NEAR_Z + p, x) for k in range(FAR)]
    for y in range(Y_SIZE)
    for p in range(NEAR_Z)
    for x in range(X_SIZE)
]


REDUCE_GROUPS = [
    [g[i] for i in ((0, 4, 2, 6, 1, 5, 3, 7), (1, 5, 3, 7, 0, 4, 2, 6))[j // X_SIZE % NEAR_Z]] for j, g in enumerate(FAR_GROUPS)
]


def exchange(blocks, groups):
    return lax.all_to_all(blocks, "seq", 0, 0, axis_index_groups=groups, tiled=True)


def row_order():
    column = lax.broadcasted_iota(jnp.int32, (WIDTH, WIDTH), 1)
    row = lax.broadcasted_iota(jnp.int32, (WIDTH, WIDTH), 0)
    half, slot = column // 128, column % 128
    near, far = slot // FAR, slot % FAR
    x = near % X_SIZE
    p = (near // X_SIZE) % NEAR_Z
    y = near // (X_SIZE * NEAR_Z)
    device = (y * Z_SIZE + far * NEAR_Z + p) * X_SIZE + x
    return (row == 2 * device + half).astype(jnp.bfloat16)


def matmul(left, right):
    return jnp.dot(left, right, preferred_element_type=jnp.float32)


def matrix_of(whole, index):
    first = whole[:, index * 512 : index * 512 + 256]
    second = whole[:, index * 512 + 256 : index * 512 + 512]
    return jnp.concatenate([first, second], axis=0)


def silu_slope(field, sigmoid_x):
    return sigmoid_x * (1.0 + field * (1.0 - sigmoid_x))


def row_rms(field):
    return jnp.sqrt(jnp.mean(field * field, axis=-1, keepdims=True) + 1e-06)


def rms_scale(field, gain):
    return field * lax.rsqrt(jnp.mean(field * field, axis=-1, keepdims=True) + 1e-06) * gain


def contract_rows(left, right):
    return lax.dot_general(
        left, right, (((0,), (0,)), ((), ())), preferred_element_type=jnp.float32
    )


def contract_columns(left, right):
    return lax.dot_general(
        left, right, (((1,), (1,)), ((), ())), preferred_element_type=jnp.float32
    )


def flat_rows(ref):
    return jnp.concatenate([ref[m, e : e + 1, :] for m in range(3) for e in range(2)], axis=1)


def send_all(stage_ref, out_hbm, sems):
    copies = [
        pltpu.make_async_copy(stage_ref, out_hbm.at[slot], sems.at[slot])
        for slot in range(out_hbm.shape[0])
    ]
    for copy in copies:
        copy.start()
    return copies


def pack_kernel(
    weights_hbm, moments_hbm, keys_hbm, values_hbm, memory_hbm, window_hbm,
    out_hbm, both_ref, weights_ref, moments_ref, memory_ref, window_ref, stage_ref, sems, out_sems,
):
    moves = (
        (weights_hbm, weights_ref),
        (moments_hbm, moments_ref),
        (keys_hbm, both_ref.at[pl.ds(0, TOKENS_HERE)]),
        (values_hbm, both_ref.at[pl.ds(TOKENS_HERE, TOKENS_HERE)]),
        (memory_hbm, memory_ref),
        (window_hbm, window_ref),
    )
    copies = [
        pltpu.make_async_copy(source, target, sems.at[i])
        for i, (source, target) in enumerate(moves)
    ]
    for copy in copies:
        copy.start()
    copies[0].wait()
    copies[1].wait()
    both = jnp.concatenate([flat_rows(weights_ref), flat_rows(moments_ref)], axis=0)
    stage_ref[...] = both.astype(jnp.bfloat16)
    for copy in send_all(stage_ref, out_hbm, out_sems) + copies[2:]:
        copy.wait()


def prepare_kernel(rate, both_ref, rates_ref, keys_out, target_out):
    keys_out[...] = matmul(both_ref[:TOKENS_HERE, :], row_order()).astype(jnp.bfloat16)
    rates = jnp.transpose(jnp.broadcast_to(rates_ref[...], (TOKENS_HERE, TOKENS_HERE)))
    scale = -(rate * jnp.concatenate([rates, rates], axis=1))
    target_out[...] = (scale * both_ref[TOKENS_HERE:, :].astype(jnp.float32)).astype(jnp.bfloat16)


def relay_kernel(line_ref, spread_ref, kept_ref):
    line = line_ref[...].astype(jnp.float32)
    weights, moments = line[:, 0, :], line[:, 1, :]
    kept_ref[:, :ROW] = weights
    kept_ref[:, ROW:] = moments
    weights = weights.astype(jnp.bfloat16)
    for slot in range(NEAR):
        spread_ref[slot] = weights


def natural_rows(slot, half):
    y, near = slot // (NEAR // Y_SIZE), slot % (NEAR // Y_SIZE)
    return pl.ds(y * 2 * Z_SIZE * X_SIZE + near * 2 + half, FAR, stride=NEAR // Y_SIZE * 2)


def natural_matrix(whole_ref, index, scratch_ref):
    for slot in range(NEAR):
        for half in range(2):
            first = (2 * index + half) * WIDTH
            part = whole_ref[slot * FAR : (slot + 1) * FAR, first : first + WIDTH]
            part = part.astype(jnp.float32)
            scratch_ref[0, natural_rows(slot, half), :] = part[:, :128]
            scratch_ref[1, natural_rows(slot, half), :] = part[:, 128:]
    return jnp.concatenate([scratch_ref[0], scratch_ref[1]], axis=1).astype(jnp.bfloat16)


def gradient_kernel(both_ref, keys_ref, target_ref, whole_ref, out_ref, down_ref, *sums):
    target_grad = target_ref[...]
    down = natural_matrix(whole_ref, 2, down_ref)
    gate_pre = matmul(keys_ref[...], matrix_of(whole_ref, 0))
    up_pre = matmul(keys_ref[...], matrix_of(whole_ref, 1))
    hidden_grad = contract_columns(target_grad, down)
    sigmoid_x = jax.nn.sigmoid(gate_pre)
    gate_act = gate_pre * sigmoid_x
    hidden = (gate_act * up_pre).astype(jnp.bfloat16)
    gate_grad = (hidden_grad * up_pre * silu_slope(gate_pre, sigmoid_x)).astype(jnp.bfloat16)
    up_grad = (hidden_grad * gate_act).astype(jnp.bfloat16)
    keys = both_ref[:TOKENS_HERE, :]
    pairs = ((hidden, target_grad), (keys, up_grad), (keys, gate_grad))
    for index, (left, right) in zip((2, 1, 0), pairs):
        total = contract_rows(left, right)
        sums[index][0] = total[:, :128]
        sums[index][1] = total[:, 128:]
        for slot in range(NEAR):
            for half in range(2):
                first = (2 * index + half) * WIDTH
                part = jnp.concatenate(
                    [sums[index][lane, natural_rows(slot, half), :] for lane in range(2)], axis=1
                )
                out_ref[slot * FAR : (slot + 1) * FAR, first : first + WIDTH] = part.astype(
                    jnp.bfloat16
                )


def near_sum_kernel(parts_ref, out_ref):
    total = parts_ref[0].astype(jnp.float32)
    for slot in range(1, NEAR):
        total += parts_ref[slot].astype(jnp.float32)
    total = total.astype(jnp.bfloat16)
    for slot in range(FAR):
        out_ref[slot] = total


def update_kernel(far_ref, decay_ref, parts_ref, kept_ref, spread_ref, own_ref, gradient_ref):
    gradient = parts_ref[0].astype(jnp.float32)
    for slot in range(1, FAR):
        gradient += parts_ref[slot].astype(jnp.float32)
    gradient_ref[...] = gradient
    decay = decay_ref[0]
    pieces = []
    for index in range(6):
        columns = slice(index * WIDTH, (index + 1) * WIDTH)
        weights = kept_ref[:, columns]
        moments = kept_ref[:, ROW + index * WIDTH : ROW + (index + 1) * WIDTH]
        candidate = weights - (decay * moments + gradient[:, columns])
        pieces.append(candidate * (row_rms(weights) / row_rms(candidate)))
    renewed = jnp.concatenate(pieces, axis=1).astype(jnp.bfloat16)
    for slot in range(NEAR):
        spread_ref[slot] = renewed
    own_ref[...] = gradient_ref[pl.ds(far_ref[0], 1), :]


def attention_kernel(
    index_ref, queries_ref, both_ref, second_ref, fourth_ref, swapped_ref, gain_ref,
    out_ref, queries_out,
):
    queries = queries_ref[...]
    queries_out[...] = matmul(queries, row_order()).astype(jnp.bfloat16)
    my_index = index_ref[0]
    query = lax.broadcasted_iota(jnp.int32, (TOKENS_HERE, TOKENS_HERE), 0)
    key = lax.broadcasted_iota(jnp.int32, (TOKENS_HERE, TOKENS_HERE), 1)
    pieces = (
        (4, fourth_ref, 0),
        (3, swapped_ref, 2 * TOKENS_HERE),
        (2, second_ref, 0),
        (1, swapped_ref, 0),
        (0, both_ref, 0),
    )
    scores = []
    for back, ref, first in pieces:
        part = contract_columns(queries, ref[first : first + TOKENS_HERE, :]) * WIDTH ** (-0.5)
        allowed = jnp.broadcast_to(my_index, key.shape) >= back
        if back == BACK:
            allowed = allowed & (key > query)
        if back == 0:
            allowed = key <= query
        scores.append(jnp.where(allowed, part, jnp.float32(-1e30)))
    scores = jnp.concatenate(scores, axis=1)
    weights = jnp.exp(scores - jnp.max(scores, axis=1, keepdims=True))
    chances = (weights / jnp.sum(weights, axis=1, keepdims=True)).astype(jnp.bfloat16)
    context = jnp.concatenate(
        [ref[first + TOKENS_HERE : first + 2 * TOKENS_HERE, :] for _, ref, first in pieces], axis=0
    )
    out_ref[...] = rms_scale(matmul(chances, context), gain_ref[...])


def recall_kernel(
    decay_ref, own_ref, weights_ref, moments_ref, queries_ref, whole_ref, attended_ref, gain_ref,
    out_hbm, weights_hbm, moments_hbm, out_ref, weights_out, moments_out, down_ref, sems,
):
    decay = decay_ref[0]
    for m in range(3):
        for e in range(2):
            first = (2 * m + e) * WIDTH
            weights = weights_ref[m, e : e + 1, :]
            moved = decay * moments_ref[m, e : e + 1, :] + own_ref[:, first : first + WIDTH]
            candidate = weights - moved
            moments_out[m, e : e + 1, :] = moved
            weights_out[m, e : e + 1, :] = candidate * (row_rms(weights) / row_rms(candidate))
    state = [
        pltpu.make_async_copy(weights_out, weights_hbm, sems.at[0]),
        pltpu.make_async_copy(moments_out, moments_hbm, sems.at[1]),
    ]
    for copy in state:
        copy.start()
    queries = queries_ref[...]
    gate_out = matmul(queries, matrix_of(whole_ref, 0))
    up_out = matmul(queries, matrix_of(whole_ref, 1))
    down = natural_matrix(whole_ref, 2, down_ref)
    inner_act = (gate_out * jax.nn.sigmoid(gate_out) * up_out).astype(jnp.bfloat16)
    recalled = matmul(inner_act, down)
    out_ref[...] = (rms_scale(recalled, gain_ref[...]) + attended_ref[...]).astype(jnp.bfloat16)
    last = pltpu.make_async_copy(out_ref, out_hbm, sems.at[2])
    last.start()
    for copy in state:
        copy.wait()
    last.wait()


VMEM = pl.BlockSpec(memory_space=pltpu.VMEM)
SMEM = pl.BlockSpec(memory_space=pltpu.SMEM)
HBM = pl.BlockSpec(memory_space=pltpu.HBM)


def stay(array):
    return pltpu.with_memory_space_constraint(array, pltpu.HBM)


def call(kernel, outputs, specs, *arrays, out_spec=VMEM, scratch=(), flops=10**8):
    single = not isinstance(outputs, list)
    shapes = [jax.ShapeDtypeStruct(*output) for output in ([outputs] if single else outputs)]
    moved = sum(array.size * array.dtype.itemsize for array in arrays)
    result = pl.pallas_call(
        kernel,
        out_shape=shapes,
        in_specs=specs,
        out_specs=out_spec if isinstance(out_spec, list) else [out_spec] * len(shapes),
        scratch_shapes=scratch,
        compiler_params=pltpu.CompilerParams(vmem_limit_bytes=8 * 2**20),
        cost_estimate=pl.CostEstimate(flops=flops, bytes_accessed=moved, transcendentals=0),
    )(*arrays)
    return result[0] if single else result


def per_device(
    queries,
    key_vectors,
    values,
    step_rates,
    fast_weights,
    momentum,
    momentum_decay,
    memory_gain,
    window_gain,
):
    seq_count = lax.axis_size("seq")
    my_index = lax.axis_index("seq")
    my_far = ((my_index // X_SIZE) % Z_SIZE) // NEAR_Z
    inner_rate = 0.1 / math.sqrt(TOKENS_HERE * seq_count)
    bf16, f32 = jnp.bfloat16, jnp.float32
    block = ((3, 2, WIDTH), f32)
    line_gain = ((1, WIDTH), f32)

    packed, both, own_weights, own_moments, memory_row, window_row = call(
        pack_kernel,
        [((FAR, 2, ROW), bf16), ((2 * TOKENS_HERE, WIDTH), bf16), block, block, line_gain, line_gain],
        [HBM] * 6,
        *map(
            stay,
            (
                fast_weights[0], momentum[0], key_vectors, values,
                memory_gain.reshape(1, WIDTH), window_gain.reshape(1, WIDTH),
            ),
        ),
        out_spec=[HBM] + [VMEM] * 5,
        scratch=[
            pltpu.VMEM((2, ROW), bf16),
            pltpu.SemaphoreType.DMA((6,)),
            pltpu.SemaphoreType.DMA((FAR,)),
        ],
    )
    line = exchange(packed, FAR_GROUPS)
    second = lax.ppermute(both, "seq", [(i, i + 2) for i in range(seq_count - 2)])
    fourth = lax.ppermute(both, "seq", [(i, i + 4) for i in range(seq_count - 4)])
    keys, target_grad = call(
        lambda *refs: prepare_kernel(inner_rate, *refs),
        [((TOKENS_HERE, WIDTH), bf16)] * 2,
        [VMEM] * 2,
        both, step_rates.reshape(1, TOKENS_HERE),
    )
    sent, kept = call(relay_kernel, [((NEAR, FAR, ROW), bf16), ((FAR, 2 * ROW), f32)], [VMEM], line)
    whole = exchange(sent, NEAR_GROUPS).reshape(seq_count, ROW)
    partial = call(
        gradient_kernel,
        ((seq_count, ROW), bf16),
        [VMEM] * 4,
        both, keys, target_grad, whole,
        scratch=[pltpu.VMEM((2, WIDTH, 128), f32)] * 4,
    )
    near_parts = exchange(partial.reshape(NEAR, FAR, ROW), NEAR_GROUPS)
    near_sum = call(near_sum_kernel, ((FAR, FAR, ROW), bf16), [VMEM], near_parts)
    far_parts = exchange(near_sum, REDUCE_GROUPS)
    odd = lax.rem(my_index, 2) == 1
    offered = jnp.where(
        odd,
        jnp.concatenate([second, fourth], axis=0),
        jnp.concatenate([both, second], axis=0),
    )
    swapped = lax.ppermute(offered, "seq", [(i, i ^ 1) for i in range(seq_count)])
    attended, queries_ordered = call(
        attention_kernel,
        [((TOKENS_HERE, WIDTH), f32), ((TOKENS_HERE, WIDTH), bf16)],
        [SMEM] + [VMEM] * 6,
        my_index.reshape(1), queries, both, second, fourth, swapped, window_row,
    )
    renewed, own_gradient = call(
        update_kernel,
        [((NEAR, FAR, ROW), bf16), ((1, ROW), f32)],
        [SMEM, SMEM] + [VMEM] * 2,
        my_far.reshape(1), momentum_decay, far_parts, kept,
        scratch=[pltpu.VMEM((FAR, ROW), f32)],
    )
    updated = exchange(renewed, NEAR_GROUPS).reshape(seq_count, ROW)
    blended, weight_new, moment_new = call(
        recall_kernel,
        [((TOKENS_HERE, WIDTH), bf16), block, block],
        [SMEM] + [VMEM] * 7,
        momentum_decay, own_gradient, own_weights, own_moments,
        queries_ordered, updated, attended, memory_row,
        out_spec=HBM,
        scratch=[
            pltpu.VMEM((TOKENS_HERE, WIDTH), bf16),
            pltpu.VMEM(*block),
            pltpu.VMEM(*block),
            pltpu.VMEM((2, WIDTH, 128), f32),
            pltpu.SemaphoreType.DMA((3,)),
        ],
    )
    return blended, weight_new[None], moment_new[None]


def solution(mesh):
    in_specs = (
        P("seq", "head"),
        P("seq", "head"),
        P("seq", "head"),
        P("seq", "head"),
        P("head", None, "seq", None),
        P("head", None, "seq", None),
        P("head"),
        P("head"),
        P("head"),
    )
    out_specs = (P("seq", "head"), P("head", None, "seq", None), P("head", None, "seq", None))
    return jax.shard_map(
        per_device, mesh=mesh, in_specs=in_specs, out_specs=out_specs, check_vma=False
    )
```

```python
import math

import jax
import jax.numpy as jnp
from jax import lax
from jax.experimental import pallas as pl
from jax.experimental.pallas import tpu as pltpu
from jax.sharding import PartitionSpec as P


WINDOW = 512
Y_SIZE, Z_SIZE, X_SIZE = 4, 16, 2
NEAR_Z = 2
FAR = Z_SIZE // NEAR_Z
NEAR = Y_SIZE * NEAR_Z * X_SIZE
WIDTH = 256
ROW = 6 * WIDTH
TOKENS_HERE = 128
BACK = WINDOW // TOKENS_HERE


def place(y, z, x):
    return (y * Z_SIZE + z) * X_SIZE + x


NEAR_GROUPS = [
    [
        place(y, k * NEAR_Z + p, x)
        for y in range(Y_SIZE)
        for p in range(NEAR_Z)
        for x in range(X_SIZE)
    ]
    for k in range(FAR)
]
FAR_GROUPS = [
    [place(y, k * NEAR_Z + p, x) for k in range(FAR)]
    for y in range(Y_SIZE)
    for p in range(NEAR_Z)
    for x in range(X_SIZE)
]


def near_at(slot):
    return (slot ^ (slot >> 1)) ^ (NEAR - 1)


NEAR_GROUPS = [[group[near_at(slot)] for slot in range(NEAR)] for group in NEAR_GROUPS]
FIRST_FAR = 5
GATHER_GROUPS = [group[FIRST_FAR:] + group[:FIRST_FAR] for group in FAR_GROUPS]
REDUCE_ORDERS = ((0, 4, 2, 6, 1, 5, 3, 7), (2, 6, 1, 5, 3, 7, 0, 4))
REDUCE_GROUPS = [
    [group[i] for i in REDUCE_ORDERS[column // X_SIZE % NEAR_Z]]
    for column, group in enumerate(FAR_GROUPS)
]


def exchange(blocks, groups):
    return lax.all_to_all(blocks, "seq", 0, 0, axis_index_groups=groups, tiled=True)


def row_order():
    column = lax.broadcasted_iota(jnp.int32, (WIDTH, WIDTH), 1)
    row = lax.broadcasted_iota(jnp.int32, (WIDTH, WIDTH), 0)
    half, slot = column // 128, column % 128
    near, far = near_at(slot // FAR), slot % FAR
    x = near % X_SIZE
    p = (near // X_SIZE) % NEAR_Z
    y = near // (X_SIZE * NEAR_Z)
    device = (y * Z_SIZE + far * NEAR_Z + p) * X_SIZE + x
    return (row == 2 * device + half).astype(jnp.bfloat16)


def matmul(left, right):
    return jnp.dot(left, right, preferred_element_type=jnp.float32)


def matrix_of(whole, index):
    first = whole[:, index * 512 : index * 512 + 256]
    second = whole[:, index * 512 + 256 : index * 512 + 512]
    return jnp.concatenate([first, second], axis=0)


def silu_slope(field, sigmoid_x):
    return sigmoid_x * (1.0 + field * (1.0 - sigmoid_x))


def row_rms(field):
    return jnp.sqrt(jnp.mean(field * field, axis=-1, keepdims=True) + 1e-06)


def rms_scale(field, gain):
    return field * lax.rsqrt(jnp.mean(field * field, axis=-1, keepdims=True) + 1e-06) * gain


def contract_rows(left, right):
    return lax.dot_general(
        left, right, (((0,), (0,)), ((), ())), preferred_element_type=jnp.float32
    )


def contract_columns(left, right):
    return lax.dot_general(
        left, right, (((1,), (1,)), ((), ())), preferred_element_type=jnp.float32
    )


def flat_rows(ref):
    return jnp.concatenate([ref[m, e : e + 1, :] for m in range(3) for e in range(2)], axis=1)


def send_all(stage_ref, out_hbm, sems):
    copies = [
        pltpu.make_async_copy(stage_ref, out_hbm.at[slot], sems.at[slot])
        for slot in range(out_hbm.shape[0])
    ]
    for copy in copies:
        copy.start()
    return copies


def pack_kernel(
    weights_hbm, moments_hbm, keys_hbm, values_hbm, memory_hbm, window_hbm, queries_hbm,
    out_hbm, both_ref, weights_ref, moments_ref, memory_ref, window_ref, queries_ref,
    stage_ref, sems, out_sems,
):
    moves = (
        (weights_hbm, weights_ref),
        (moments_hbm, moments_ref),
        (keys_hbm, both_ref.at[pl.ds(0, TOKENS_HERE)]),
        (values_hbm, both_ref.at[pl.ds(TOKENS_HERE, TOKENS_HERE)]),
        (memory_hbm, memory_ref),
        (window_hbm, window_ref),
        (queries_hbm, queries_ref),
    )
    copies = [
        pltpu.make_async_copy(source, target, sems.at[i])
        for i, (source, target) in enumerate(moves)
    ]
    for copy in copies:
        copy.start()
    copies[0].wait()
    copies[1].wait()
    both = jnp.concatenate([flat_rows(weights_ref), flat_rows(moments_ref)], axis=0)
    stage_ref[...] = both.astype(jnp.bfloat16)
    for copy in send_all(stage_ref, out_hbm, out_sems) + copies[2:]:
        copy.wait()


def prepare_kernel(rate, both_ref, rates_ref, queries_ref, keys_out, target_out, queries_out):
    order = row_order()
    keys_out[...] = matmul(both_ref[:TOKENS_HERE, :], order).astype(jnp.bfloat16)
    queries_out[...] = matmul(queries_ref[...], order).astype(jnp.bfloat16)
    rates = jnp.transpose(jnp.broadcast_to(rates_ref[...], (TOKENS_HERE, TOKENS_HERE)))
    scale = -(rate * jnp.concatenate([rates, rates], axis=1))
    target_out[...] = (scale * both_ref[TOKENS_HERE:, :].astype(jnp.float32)).astype(jnp.bfloat16)


def relay_kernel(line_ref, spread_ref, kept_ref):
    first = FAR - FIRST_FAR
    line = jnp.concatenate([line_ref[first:], line_ref[:first]], axis=0).astype(jnp.float32)
    weights, moments = line[:, 0, :], line[:, 1, :]
    kept_ref[:, :ROW] = weights
    kept_ref[:, ROW:] = moments
    weights = weights.astype(jnp.bfloat16)
    for slot in range(NEAR):
        spread_ref[slot] = weights


def natural_rows(slot, half):
    y, near = near_at(slot) // (NEAR // Y_SIZE), near_at(slot) % (NEAR // Y_SIZE)
    return pl.ds(y * 2 * Z_SIZE * X_SIZE + near * 2 + half, FAR, stride=NEAR // Y_SIZE * 2)


def natural_matrix(whole_ref, index, scratch_ref):
    for slot in range(NEAR):
        for half in range(2):
            first = (2 * index + half) * WIDTH
            part = whole_ref[slot * FAR : (slot + 1) * FAR, first : first + WIDTH]
            part = part.astype(jnp.float32)
            scratch_ref[0, natural_rows(slot, half), :] = part[:, :128]
            scratch_ref[1, natural_rows(slot, half), :] = part[:, 128:]
    return jnp.concatenate([scratch_ref[0], scratch_ref[1]], axis=1).astype(jnp.bfloat16)


def gradient_kernel(both_ref, keys_ref, target_ref, whole_ref, out_ref, down_ref, *sums):
    target_grad = target_ref[...]
    down = natural_matrix(whole_ref, 2, down_ref)
    gate_pre = matmul(keys_ref[...], matrix_of(whole_ref, 0))
    up_pre = matmul(keys_ref[...], matrix_of(whole_ref, 1))
    hidden_grad = contract_columns(target_grad, down)
    sigmoid_x = jax.nn.sigmoid(gate_pre)
    gate_act = gate_pre * sigmoid_x
    hidden = (gate_act * up_pre).astype(jnp.bfloat16)
    gate_grad = (hidden_grad * up_pre * silu_slope(gate_pre, sigmoid_x)).astype(jnp.bfloat16)
    up_grad = (hidden_grad * gate_act).astype(jnp.bfloat16)
    keys = both_ref[:TOKENS_HERE, :]
    pairs = ((hidden, target_grad), (keys, up_grad), (keys, gate_grad))
    for index, (left, right) in zip((2, 1, 0), pairs):
        total = contract_rows(left, right)
        sums[index][0] = total[:, :128]
        sums[index][1] = total[:, 128:]
        for slot in range(NEAR):
            for half in range(2):
                first = (2 * index + half) * WIDTH
                part = jnp.concatenate(
                    [sums[index][lane, natural_rows(slot, half), :] for lane in range(2)], axis=1
                )
                out_ref[slot * FAR : (slot + 1) * FAR, first : first + WIDTH] = part.astype(
                    jnp.bfloat16
                )


def near_sum_kernel(parts_ref, out_ref):
    total = parts_ref[0].astype(jnp.float32)
    for slot in range(1, NEAR):
        total += parts_ref[slot].astype(jnp.float32)
    total = total.astype(jnp.bfloat16)
    for slot in range(FAR):
        out_ref[slot] = total


def update_kernel(far_ref, decay_ref, parts_ref, kept_ref, spread_ref, own_ref, gradient_ref):
    gradient = parts_ref[0].astype(jnp.float32)
    for slot in range(1, FAR):
        gradient += parts_ref[slot].astype(jnp.float32)
    gradient_ref[...] = gradient
    decay = decay_ref[0]
    pieces = []
    for index in range(6):
        columns = slice(index * WIDTH, (index + 1) * WIDTH)
        weights = kept_ref[:, columns]
        moments = kept_ref[:, ROW + index * WIDTH : ROW + (index + 1) * WIDTH]
        candidate = weights - (decay * moments + gradient[:, columns])
        pieces.append(candidate * (row_rms(weights) / row_rms(candidate)))
    renewed = jnp.concatenate(pieces, axis=1).astype(jnp.bfloat16)
    for slot in range(NEAR):
        spread_ref[slot] = renewed
    own_ref[...] = gradient_ref[pl.ds(far_ref[0], 1), :]


def attention_kernel(
    index_ref, queries_ref, both_ref, second_ref, fourth_ref, swapped_ref, gain_ref,
    out_ref,
):
    queries = queries_ref[...]
    my_index = index_ref[0]
    query = lax.broadcasted_iota(jnp.int32, (TOKENS_HERE, TOKENS_HERE), 0)
    key = lax.broadcasted_iota(jnp.int32, (TOKENS_HERE, TOKENS_HERE), 1)
    pieces = (
        (4, fourth_ref, 0),
        (3, swapped_ref, 2 * TOKENS_HERE),
        (2, second_ref, 0),
        (1, swapped_ref, 0),
        (0, both_ref, 0),
    )
    scores = []
    for back, ref, first in pieces:
        part = contract_columns(queries, ref[first : first + TOKENS_HERE, :]) * WIDTH ** (-0.5)
        allowed = jnp.broadcast_to(my_index, key.shape) >= back
        if back == BACK:
            allowed = allowed & (key > query)
        if back == 0:
            allowed = key <= query
        scores.append(jnp.where(allowed, part, jnp.float32(-1e30)))
    scores = jnp.concatenate(scores, axis=1)
    weights = jnp.exp(scores - jnp.max(scores, axis=1, keepdims=True))
    chances = (weights / jnp.sum(weights, axis=1, keepdims=True)).astype(jnp.bfloat16)
    context = jnp.concatenate(
        [ref[first + TOKENS_HERE : first + 2 * TOKENS_HERE, :] for _, ref, first in pieces], axis=0
    )
    out_ref[...] = rms_scale(matmul(chances, context), gain_ref[...])


def recall_kernel(
    decay_ref, own_ref, weights_ref, moments_ref, queries_ref, whole_ref, attended_ref, gain_ref,
    out_hbm, weights_hbm, moments_hbm, out_ref, weights_out, moments_out, down_ref, sems,
):
    decay = decay_ref[0]
    for m in range(3):
        for e in range(2):
            first = (2 * m + e) * WIDTH
            weights = weights_ref[m, e : e + 1, :]
            moved = decay * moments_ref[m, e : e + 1, :] + own_ref[:, first : first + WIDTH]
            candidate = weights - moved
            moments_out[m, e : e + 1, :] = moved
            weights_out[m, e : e + 1, :] = candidate * (row_rms(weights) / row_rms(candidate))
    state = [
        pltpu.make_async_copy(weights_out, weights_hbm, sems.at[0]),
        pltpu.make_async_copy(moments_out, moments_hbm, sems.at[1]),
    ]
    for copy in state:
        copy.start()
    queries = queries_ref[...]
    gate_out = matmul(queries, matrix_of(whole_ref, 0))
    up_out = matmul(queries, matrix_of(whole_ref, 1))
    down = natural_matrix(whole_ref, 2, down_ref)
    inner_act = (gate_out * jax.nn.sigmoid(gate_out) * up_out).astype(jnp.bfloat16)
    recalled = matmul(inner_act, down)
    out_ref[...] = (rms_scale(recalled, gain_ref[...]) + attended_ref[...]).astype(jnp.bfloat16)
    last = pltpu.make_async_copy(out_ref, out_hbm, sems.at[2])
    last.start()
    for copy in state:
        copy.wait()
    last.wait()


VMEM = pl.BlockSpec(memory_space=pltpu.VMEM)
SMEM = pl.BlockSpec(memory_space=pltpu.SMEM)
HBM = pl.BlockSpec(memory_space=pltpu.HBM)


def stay(array):
    return pltpu.with_memory_space_constraint(array, pltpu.HBM)


def call(kernel, outputs, specs, *arrays, out_spec=VMEM, scratch=(), flops=10**8):
    single = not isinstance(outputs, list)
    shapes = [jax.ShapeDtypeStruct(*output) for output in ([outputs] if single else outputs)]
    moved = sum(array.size * array.dtype.itemsize for array in arrays)
    result = pl.pallas_call(
        kernel,
        out_shape=shapes,
        in_specs=specs,
        out_specs=out_spec if isinstance(out_spec, list) else [out_spec] * len(shapes),
        scratch_shapes=scratch,
        compiler_params=pltpu.CompilerParams(vmem_limit_bytes=8 * 2**20),
        cost_estimate=pl.CostEstimate(flops=flops, bytes_accessed=moved, transcendentals=0),
    )(*arrays)
    return result[0] if single else result


def per_device(
    queries,
    key_vectors,
    values,
    step_rates,
    fast_weights,
    momentum,
    momentum_decay,
    memory_gain,
    window_gain,
):
    seq_count = lax.axis_size("seq")
    my_index = lax.axis_index("seq")
    my_far = ((my_index // X_SIZE) % Z_SIZE) // NEAR_Z
    inner_rate = 0.1 / math.sqrt(TOKENS_HERE * seq_count)
    bf16, f32 = jnp.bfloat16, jnp.float32
    block = ((3, 2, WIDTH), f32)
    line_gain = ((1, WIDTH), f32)

    packed, both, own_weights, own_moments, memory_row, window_row, own_queries = call(
        pack_kernel,
        [((FAR, 2, ROW), bf16), ((2 * TOKENS_HERE, WIDTH), bf16), block, block, line_gain, line_gain, ((TOKENS_HERE, WIDTH), bf16)],
        [HBM] * 7,
        *map(
            stay,
            (
                fast_weights[0], momentum[0], key_vectors, values,
                memory_gain.reshape(1, WIDTH), window_gain.reshape(1, WIDTH),
                queries,
            ),
        ),
        out_spec=[HBM] + [VMEM] * 6,
        scratch=[
            pltpu.VMEM((2, ROW), bf16),
            pltpu.SemaphoreType.DMA((7,)),
            pltpu.SemaphoreType.DMA((FAR,)),
        ],
    )
    line = exchange(packed, GATHER_GROUPS)
    second = lax.ppermute(both, "seq", [(i, i + 2) for i in range(seq_count - 2)])
    fourth = lax.ppermute(both, "seq", [(i, i + 4) for i in range(seq_count - 4)])
    keys, target_grad, queries_ordered = call(
        lambda *refs: prepare_kernel(inner_rate, *refs),
        [((TOKENS_HERE, WIDTH), bf16)] * 3,
        [VMEM] * 3,
        both, step_rates.reshape(1, TOKENS_HERE), own_queries,
    )
    sent, kept = call(relay_kernel, [((NEAR, FAR, ROW), bf16), ((FAR, 2 * ROW), f32)], [VMEM], line)
    whole = exchange(sent, NEAR_GROUPS).reshape(seq_count, ROW)
    partial = call(
        gradient_kernel,
        ((seq_count, ROW), bf16),
        [VMEM] * 4,
        both, keys, target_grad, whole,
        scratch=[pltpu.VMEM((2, WIDTH, 128), f32)] * 4,
    )
    near_parts = exchange(partial.reshape(NEAR, FAR, ROW), NEAR_GROUPS)
    near_sum = call(near_sum_kernel, ((FAR, FAR, ROW), bf16), [VMEM], near_parts)
    far_parts = exchange(near_sum, REDUCE_GROUPS)
    odd = lax.rem(my_index, 2) == 1
    offered = jnp.where(
        odd,
        jnp.concatenate([second, fourth], axis=0),
        jnp.concatenate([both, second], axis=0),
    )
    swapped = lax.ppermute(offered, "seq", [(i, i ^ 1) for i in range(seq_count)])
    attended = call(
        attention_kernel,
        ((TOKENS_HERE, WIDTH), f32),
        [SMEM] + [VMEM] * 6,
        my_index.reshape(1), own_queries, both, second, fourth, swapped, window_row,
    )
    renewed, own_gradient = call(
        update_kernel,
        [((NEAR, FAR, ROW), bf16), ((1, ROW), f32)],
        [SMEM, SMEM] + [VMEM] * 2,
        my_far.reshape(1), momentum_decay, far_parts, kept,
        scratch=[pltpu.VMEM((FAR, ROW), f32)],
    )
    updated = exchange(renewed, NEAR_GROUPS).reshape(seq_count, ROW)
    blended, weight_new, moment_new = call(
        recall_kernel,
        [((TOKENS_HERE, WIDTH), bf16), block, block],
        [SMEM] + [VMEM] * 7,
        momentum_decay, own_gradient, own_weights, own_moments,
        queries_ordered, updated, attended, memory_row,
        out_spec=HBM,
        scratch=[
            pltpu.VMEM((TOKENS_HERE, WIDTH), bf16),
            pltpu.VMEM(*block),
            pltpu.VMEM(*block),
            pltpu.VMEM((2, WIDTH, 128), f32),
            pltpu.SemaphoreType.DMA((3,)),
        ],
    )
    return blended, weight_new[None], moment_new[None]


def solution(mesh):
    in_specs = (
        P("seq", "head"),
        P("seq", "head"),
        P("seq", "head"),
        P("seq", "head"),
        P("head", None, "seq", None),
        P("head", None, "seq", None),
        P("head"),
        P("head"),
        P("head"),
    )
    out_specs = (P("seq", "head"), P("head", None, "seq", None), P("head", None, "seq", None))
    return jax.shard_map(
        per_device, mesh=mesh, in_specs=in_specs, out_specs=out_specs, check_vma=False
    )
```

```python
import math

import jax
import jax.numpy as jnp
from jax import lax
from jax.experimental import pallas as pl
from jax.experimental.pallas import tpu as pltpu
from jax.sharding import PartitionSpec as P


WINDOW = 512
Y_SIZE, Z_SIZE, X_SIZE = 4, 16, 2
NEAR_Z = 2
FAR = Z_SIZE // NEAR_Z
NEAR = Y_SIZE * NEAR_Z * X_SIZE
WIDTH = 256
ROW = 6 * WIDTH
TOKENS_HERE = 128
BACK = WINDOW // TOKENS_HERE


def place(y, z, x):
    return (y * Z_SIZE + z) * X_SIZE + x


NEAR_GROUPS = [
    [
        place(y, k * NEAR_Z + p, x)
        for y in range(Y_SIZE)
        for p in range(NEAR_Z)
        for x in range(X_SIZE)
    ]
    for k in range(FAR)
]
FAR_GROUPS = [
    [place(y, k * NEAR_Z + p, x) for k in range(FAR)]
    for y in range(Y_SIZE)
    for p in range(NEAR_Z)
    for x in range(X_SIZE)
]


def near_at(slot):
    return (slot ^ (slot >> 1)) ^ (NEAR - 1)


NEAR_GROUPS = [[group[near_at(slot)] for slot in range(NEAR)] for group in NEAR_GROUPS]
FIRST_FAR = 5
GATHER_GROUPS = [group[FIRST_FAR:] + group[:FIRST_FAR] for group in FAR_GROUPS]
REDUCE_ORDERS = ((0, 4, 2, 6, 1, 5, 3, 7), (2, 6, 1, 5, 3, 7, 0, 4))
REDUCE_GROUPS = [
    [group[i] for i in REDUCE_ORDERS[column // X_SIZE % NEAR_Z]]
    for column, group in enumerate(FAR_GROUPS)
]


def exchange(blocks, groups):
    return lax.all_to_all(blocks, "seq", 0, 0, axis_index_groups=groups, tiled=True)


def row_order():
    column = lax.broadcasted_iota(jnp.int32, (WIDTH, WIDTH), 1)
    row = lax.broadcasted_iota(jnp.int32, (WIDTH, WIDTH), 0)
    half, slot = column // 128, column % 128
    near, far = near_at(slot // FAR), slot % FAR
    x = near % X_SIZE
    p = (near // X_SIZE) % NEAR_Z
    y = near // (X_SIZE * NEAR_Z)
    device = (y * Z_SIZE + far * NEAR_Z + p) * X_SIZE + x
    return (row == 2 * device + half).astype(jnp.bfloat16)


def matmul(left, right):
    return jnp.dot(left, right, preferred_element_type=jnp.float32)


def matrix_of(whole, index):
    first = whole[:, index * 512 : index * 512 + 256]
    second = whole[:, index * 512 + 256 : index * 512 + 512]
    return jnp.concatenate([first, second], axis=0)


def silu_slope(field, sigmoid_x):
    return sigmoid_x * (1.0 + field * (1.0 - sigmoid_x))


def row_rms(field):
    return jnp.sqrt(jnp.mean(field * field, axis=-1, keepdims=True) + 1e-06)


def rms_scale(field, gain):
    return field * lax.rsqrt(jnp.mean(field * field, axis=-1, keepdims=True) + 1e-06) * gain


def contract_rows(left, right):
    return lax.dot_general(
        left, right, (((0,), (0,)), ((), ())), preferred_element_type=jnp.float32
    )


def contract_columns(left, right):
    return lax.dot_general(
        left, right, (((1,), (1,)), ((), ())), preferred_element_type=jnp.float32
    )


def flat_rows(ref):
    return jnp.concatenate([ref[m, e : e + 1, :] for m in range(3) for e in range(2)], axis=1)


def send_all(stage_ref, out_hbm, sems):
    copies = [
        pltpu.make_async_copy(stage_ref, out_hbm.at[slot], sems.at[slot])
        for slot in range(out_hbm.shape[0])
    ]
    for copy in copies:
        copy.start()
    return copies


def pack_kernel(
    weights_hbm, moments_hbm, keys_hbm, values_hbm, memory_hbm, window_hbm,
    out_hbm, both_ref, weights_ref, moments_ref, memory_ref, window_ref, stage_ref, sems, out_sems,
):
    moves = (
        (weights_hbm, weights_ref),
        (moments_hbm, moments_ref),
        (keys_hbm, both_ref.at[pl.ds(0, TOKENS_HERE)]),
        (values_hbm, both_ref.at[pl.ds(TOKENS_HERE, TOKENS_HERE)]),
        (memory_hbm, memory_ref),
        (window_hbm, window_ref),
    )
    copies = [
        pltpu.make_async_copy(source, target, sems.at[i])
        for i, (source, target) in enumerate(moves)
    ]
    for copy in copies:
        copy.start()
    copies[0].wait()
    copies[1].wait()
    both = jnp.concatenate([flat_rows(weights_ref), flat_rows(moments_ref)], axis=0)
    stage_ref[...] = both.astype(jnp.bfloat16)
    for copy in send_all(stage_ref, out_hbm, out_sems) + copies[2:]:
        copy.wait()


def prepare_kernel(rate, both_ref, rates_ref, keys_out, target_out):
    keys_out[...] = matmul(both_ref[:TOKENS_HERE, :], row_order()).astype(jnp.bfloat16)
    rates = jnp.transpose(jnp.broadcast_to(rates_ref[...], (TOKENS_HERE, TOKENS_HERE)))
    scale = -(rate * jnp.concatenate([rates, rates], axis=1))
    target_out[...] = (scale * both_ref[TOKENS_HERE:, :].astype(jnp.float32)).astype(jnp.bfloat16)


def relay_kernel(line_ref, spread_ref, kept_ref):
    first = FAR - FIRST_FAR
    line = jnp.concatenate([line_ref[first:], line_ref[:first]], axis=0).astype(jnp.float32)
    weights, moments = line[:, 0, :], line[:, 1, :]
    kept_ref[:, :ROW] = weights
    kept_ref[:, ROW:] = moments
    weights = weights.astype(jnp.bfloat16)
    for slot in range(NEAR):
        spread_ref[slot] = weights


def natural_rows(slot, half):
    y, near = near_at(slot) // (NEAR // Y_SIZE), near_at(slot) % (NEAR // Y_SIZE)
    return pl.ds(y * 2 * Z_SIZE * X_SIZE + near * 2 + half, FAR, stride=NEAR // Y_SIZE * 2)


def natural_matrix(whole_ref, index, scratch_ref):
    for slot in range(NEAR):
        for half in range(2):
            first = (2 * index + half) * WIDTH
            part = whole_ref[slot * FAR : (slot + 1) * FAR, first : first + WIDTH]
            part = part.astype(jnp.float32)
            scratch_ref[0, natural_rows(slot, half), :] = part[:, :128]
            scratch_ref[1, natural_rows(slot, half), :] = part[:, 128:]
    return jnp.concatenate([scratch_ref[0], scratch_ref[1]], axis=1).astype(jnp.bfloat16)


def gradient_kernel(both_ref, keys_ref, target_ref, whole_ref, out_ref, down_ref, *sums):
    target_grad = target_ref[...]
    down = natural_matrix(whole_ref, 2, down_ref)
    gate_pre = matmul(keys_ref[...], matrix_of(whole_ref, 0))
    up_pre = matmul(keys_ref[...], matrix_of(whole_ref, 1))
    hidden_grad = contract_columns(target_grad, down)
    sigmoid_x = jax.nn.sigmoid(gate_pre)
    gate_act = gate_pre * sigmoid_x
    hidden = (gate_act * up_pre).astype(jnp.bfloat16)
    gate_grad = (hidden_grad * up_pre * silu_slope(gate_pre, sigmoid_x)).astype(jnp.bfloat16)
    up_grad = (hidden_grad * gate_act).astype(jnp.bfloat16)
    keys = both_ref[:TOKENS_HERE, :]
    pairs = ((hidden, target_grad), (keys, up_grad), (keys, gate_grad))
    for index, (left, right) in zip((2, 1, 0), pairs):
        total = contract_rows(left, right)
        sums[index][0] = total[:, :128]
        sums[index][1] = total[:, 128:]
        for slot in range(NEAR):
            for half in range(2):
                first = (2 * index + half) * WIDTH
                part = jnp.concatenate(
                    [sums[index][lane, natural_rows(slot, half), :] for lane in range(2)], axis=1
                )
                out_ref[slot * FAR : (slot + 1) * FAR, first : first + WIDTH] = part.astype(
                    jnp.bfloat16
                )


def near_sum_kernel(parts_ref, out_ref):
    total = parts_ref[0].astype(jnp.float32)
    for slot in range(1, NEAR):
        total += parts_ref[slot].astype(jnp.float32)
    total = total.astype(jnp.bfloat16)
    for slot in range(FAR):
        out_ref[slot] = total


def update_kernel(far_ref, decay_ref, parts_ref, kept_ref, spread_ref, own_ref, gradient_ref):
    gradient = parts_ref[0].astype(jnp.float32)
    for slot in range(1, FAR):
        gradient += parts_ref[slot].astype(jnp.float32)
    gradient_ref[...] = gradient
    decay = decay_ref[0]
    pieces = []
    for index in range(6):
        columns = slice(index * WIDTH, (index + 1) * WIDTH)
        weights = kept_ref[:, columns]
        moments = kept_ref[:, ROW + index * WIDTH : ROW + (index + 1) * WIDTH]
        candidate = weights - (decay * moments + gradient[:, columns])
        pieces.append(candidate * (row_rms(weights) / row_rms(candidate)))
    renewed = jnp.concatenate(pieces, axis=1).astype(jnp.bfloat16)
    for slot in range(NEAR):
        spread_ref[slot] = renewed
    own_ref[...] = gradient_ref[pl.ds(far_ref[0], 1), :]


def attention_kernel(
    index_ref, queries_ref, both_ref, second_ref, fourth_ref, swapped_ref, gain_ref,
    out_ref, queries_out,
):
    queries = queries_ref[...]
    queries_out[...] = matmul(queries, row_order()).astype(jnp.bfloat16)
    my_index = index_ref[0]
    query = lax.broadcasted_iota(jnp.int32, (TOKENS_HERE, TOKENS_HERE), 0)
    key = lax.broadcasted_iota(jnp.int32, (TOKENS_HERE, TOKENS_HERE), 1)
    pieces = (
        (4, fourth_ref, 0),
        (3, swapped_ref, 2 * TOKENS_HERE),
        (2, second_ref, 0),
        (1, swapped_ref, 0),
        (0, both_ref, 0),
    )
    scores = []
    for back, ref, first in pieces:
        part = contract_columns(queries, ref[first : first + TOKENS_HERE, :]) * WIDTH ** (-0.5)
        allowed = jnp.broadcast_to(my_index, key.shape) >= back
        if back == BACK:
            allowed = allowed & (key > query)
        if back == 0:
            allowed = key <= query
        scores.append(jnp.where(allowed, part, jnp.float32(-1e30)))
    scores = jnp.concatenate(scores, axis=1)
    weights = jnp.exp(scores - jnp.max(scores, axis=1, keepdims=True))
    chances = (weights * (1.0 / jnp.sum(weights, axis=1, keepdims=True))).astype(jnp.bfloat16)
    context = jnp.concatenate(
        [ref[first + TOKENS_HERE : first + 2 * TOKENS_HERE, :] for _, ref, first in pieces], axis=0
    )
    out_ref[...] = rms_scale(matmul(chances, context), gain_ref[...])


def recall_kernel(
    decay_ref, own_ref, weights_ref, moments_ref, queries_ref, whole_ref, attended_ref, gain_ref,
    out_hbm, weights_hbm, moments_hbm, out_ref, weights_out, moments_out, down_ref, sems,
):
    decay = decay_ref[0]
    for m in range(3):
        for e in range(2):
            first = (2 * m + e) * WIDTH
            weights = weights_ref[m, e : e + 1, :]
            moved = decay * moments_ref[m, e : e + 1, :] + own_ref[:, first : first + WIDTH]
            candidate = weights - moved
            moments_out[m, e : e + 1, :] = moved
            weights_out[m, e : e + 1, :] = candidate * (row_rms(weights) / row_rms(candidate))
    state = [
        pltpu.make_async_copy(weights_out, weights_hbm, sems.at[0]),
        pltpu.make_async_copy(moments_out, moments_hbm, sems.at[1]),
    ]
    for copy in state:
        copy.start()
    queries = queries_ref[...]
    gate_out = matmul(queries, matrix_of(whole_ref, 0))
    up_out = matmul(queries, matrix_of(whole_ref, 1))
    down = natural_matrix(whole_ref, 2, down_ref)
    inner_act = (gate_out * jax.nn.sigmoid(gate_out) * up_out).astype(jnp.bfloat16)
    recalled = matmul(inner_act, down)
    out_ref[...] = (rms_scale(recalled, gain_ref[...]) + attended_ref[...]).astype(jnp.bfloat16)
    last = pltpu.make_async_copy(out_ref, out_hbm, sems.at[2])
    last.start()
    for copy in state:
        copy.wait()
    last.wait()


VMEM = pl.BlockSpec(memory_space=pltpu.VMEM)
SMEM = pl.BlockSpec(memory_space=pltpu.SMEM)
HBM = pl.BlockSpec(memory_space=pltpu.HBM)


def stay(array):
    return pltpu.with_memory_space_constraint(array, pltpu.HBM)


def call(kernel, outputs, specs, *arrays, out_spec=VMEM, scratch=(), flops=10**8):
    single = not isinstance(outputs, list)
    shapes = [jax.ShapeDtypeStruct(*output) for output in ([outputs] if single else outputs)]
    moved = sum(array.size * array.dtype.itemsize for array in arrays)
    result = pl.pallas_call(
        kernel,
        out_shape=shapes,
        in_specs=specs,
        out_specs=out_spec if isinstance(out_spec, list) else [out_spec] * len(shapes),
        scratch_shapes=scratch,
        compiler_params=pltpu.CompilerParams(vmem_limit_bytes=8 * 2**20),
        cost_estimate=pl.CostEstimate(flops=flops, bytes_accessed=moved, transcendentals=0),
    )(*arrays)
    return result[0] if single else result


def per_device(
    queries,
    key_vectors,
    values,
    step_rates,
    fast_weights,
    momentum,
    momentum_decay,
    memory_gain,
    window_gain,
):
    seq_count = lax.axis_size("seq")
    my_index = lax.axis_index("seq")
    my_far = ((my_index // X_SIZE) % Z_SIZE) // NEAR_Z
    inner_rate = 0.1 / math.sqrt(TOKENS_HERE * seq_count)
    bf16, f32 = jnp.bfloat16, jnp.float32
    block = ((3, 2, WIDTH), f32)
    line_gain = ((1, WIDTH), f32)

    packed, both, own_weights, own_moments, memory_row, window_row = call(
        pack_kernel,
        [((FAR, 2, ROW), bf16), ((2 * TOKENS_HERE, WIDTH), bf16), block, block, line_gain, line_gain],
        [HBM] * 6,
        *map(
            stay,
            (
                fast_weights[0], momentum[0], key_vectors, values,
                memory_gain.reshape(1, WIDTH), window_gain.reshape(1, WIDTH),
            ),
        ),
        out_spec=[HBM] + [VMEM] * 5,
        scratch=[
            pltpu.VMEM((2, ROW), bf16),
            pltpu.SemaphoreType.DMA((6,)),
            pltpu.SemaphoreType.DMA((FAR,)),
        ],
    )
    line = exchange(packed, GATHER_GROUPS)
    second = lax.ppermute(both, "seq", [(i, i + 2) for i in range(seq_count - 2)])
    fourth = lax.ppermute(both, "seq", [(i, i + 4) for i in range(seq_count - 4)])
    keys, target_grad = call(
        lambda *refs: prepare_kernel(inner_rate, *refs),
        [((TOKENS_HERE, WIDTH), bf16)] * 2,
        [VMEM] * 2,
        both, step_rates.reshape(1, TOKENS_HERE),
    )
    sent, kept = call(relay_kernel, [((NEAR, FAR, ROW), bf16), ((FAR, 2 * ROW), f32)], [VMEM], line)
    whole = exchange(sent, NEAR_GROUPS).reshape(seq_count, ROW)
    partial = call(
        gradient_kernel,
        ((seq_count, ROW), bf16),
        [VMEM] * 4,
        both, keys, target_grad, whole,
        scratch=[pltpu.VMEM((2, WIDTH, 128), f32)] * 4,
    )
    near_parts = exchange(partial.reshape(NEAR, FAR, ROW), NEAR_GROUPS)
    near_sum = call(near_sum_kernel, ((FAR, FAR, ROW), bf16), [VMEM], near_parts)
    far_parts = exchange(near_sum, REDUCE_GROUPS)
    odd = lax.rem(my_index, 2) == 1
    offered = jnp.where(
        odd,
        jnp.concatenate([second, fourth], axis=0),
        jnp.concatenate([both, second], axis=0),
    )
    swapped = lax.ppermute(offered, "seq", [(i, i ^ 1) for i in range(seq_count)])
    attended, queries_ordered = call(
        attention_kernel,
        [((TOKENS_HERE, WIDTH), f32), ((TOKENS_HERE, WIDTH), bf16)],
        [SMEM] + [VMEM] * 6,
        my_index.reshape(1), queries, both, second, fourth, swapped, window_row,
    )
    renewed, own_gradient = call(
        update_kernel,
        [((NEAR, FAR, ROW), bf16), ((1, ROW), f32)],
        [SMEM, SMEM] + [VMEM] * 2,
        my_far.reshape(1), momentum_decay, far_parts, kept,
        scratch=[pltpu.VMEM((FAR, ROW), f32)],
    )
    updated = exchange(renewed, NEAR_GROUPS).reshape(seq_count, ROW)
    blended, weight_new, moment_new = call(
        recall_kernel,
        [((TOKENS_HERE, WIDTH), bf16), block, block],
        [SMEM] + [VMEM] * 7,
        momentum_decay, own_gradient, own_weights, own_moments,
        queries_ordered, updated, attended, memory_row,
        out_spec=HBM,
        scratch=[
            pltpu.VMEM((TOKENS_HERE, WIDTH), bf16),
            pltpu.VMEM(*block),
            pltpu.VMEM(*block),
            pltpu.VMEM((2, WIDTH, 128), f32),
            pltpu.SemaphoreType.DMA((3,)),
        ],
    )
    return blended, weight_new[None], moment_new[None]


def solution(mesh):
    in_specs = (
        P("seq", "head"),
        P("seq", "head"),
        P("seq", "head"),
        P("seq", "head"),
        P("head", None, "seq", None),
        P("head", None, "seq", None),
        P("head"),
        P("head"),
        P("head"),
    )
    out_specs = (P("seq", "head"), P("head", None, "seq", None), P("head", None, "seq", None))
    return jax.shard_map(
        per_device, mesh=mesh, in_specs=in_specs, out_specs=out_specs, check_vma=False
    )
```
